128 devices in a mesh: rows: 32 (over y, x, core), cols: 4 (over z).
Axes of the slice: x: 4, y: 4, z: 4, core: 2. Of those that a mesh axis runs over, the one named last changes fastest.
Arguments:
- factor_rows: bfloat16 [65536, 128], P('rows'), may hold values from -2 to 2
- factor_cols: bfloat16 [262144, 128], P(('rows', 'cols')), may hold values from -2 to 2
- observed: bfloat16 [16384, 256, 256], P(('rows', 'cols')), may hold values from -6 to 6
- tile_row: int32 [16384], P(('rows', 'cols')), may hold values from 0 to 7
- tile_owner: int32 [16384, 1], P(('rows', 'cols')), may hold values from 0 to 127; in each aligned block of 128 rows (0 to 127, 128 to 255, ...) at most 2 rows name the same one
- tile_sub: int32 [16384], P(('rows', 'cols')), may hold values from 0 to 7
Outputs:
- rows_new: float32 [65536, 128], P('rows')
- cols_new: float32 [262144, 128], P(('rows', 'cols'))
The draws below stay inside these ranges and needn't reach their ends.
Inputs may be any that keep to these rules, and one draw needn't show every extreme that they name: `tile_owner`: among the 128 tiles of one device at most 2 have the same owner; in every draw some device has exactly 2 tiles of one owner.
All inputs are finite; a program needn't handle non-finite values.
Results may differ from the reference program's by a relative error of at most 0.0014.
Values may be sent and summed in bfloat16 or wider, within the bound.
A program may use at most 192 MiB of HBM per device.

```python
import math
import jax
import jax.numpy as jnp
import numpy as np
from jax import lax

K = 128
TB = 256
TILES_DEV = 128
RBD = 8
CAP = 2
CBD = 8
TILES = 16384
ROWS_TOTAL = 65536
COLS_TOTAL = 262144
N_ROWS = 32
N_COLS = 4
DEVICES = 128


def place_ends(entries, rng, smallest, top_value):
    longest = entries.shape.index(max(entries.shape))
    spots = []
    for shift in (0, 1):
        where = [jax.random.randint(jax.random.fold_in(rng, axis), (), 0, length) for axis, length in enumerate(entries.shape)]
        where[longest] = (where[longest] + shift) % entries.shape[longest]
        spots.append(tuple(where))
    return entries.at[spots[0]].set(smallest).at[spots[1]].set(top_value)


def block_scale(key, shape, cuts, least, top_value):
    def one(position, blocks):
        draws = jax.random.uniform(jax.random.fold_in(jax.random.fold_in(key, 6), position), (blocks,), jnp.float32, least / len(cuts), top_value / len(cuts))
        return jnp.repeat(jnp.exp(draws), shape[position] // blocks).reshape((-1,) + (1,) * (len(shape) - position - 1))

    factor_of = one(*cuts[0])
    for cut in cuts[1:]:
        factor_of = factor_of * one(*cut)
    return factor_of


def routed_block(own_key, own, number, rows, count, top, reach, lean):
    ranking = jax.random.permutation(own_key, count)
    packed, ordinary = load_shares(count, rows * top, reach, lean, True), load_shares(count, rows * top, reach, lean, False)
    places = jnp.arange(count)

    def named(lengths, turn):
        used = int((lengths > 0).sum())
        fixed = max(1, used // 4)
        passed = fixed + (places - fixed + turn * (used - fixed)) % max(1, count - fixed)
        return jnp.zeros((count,), jnp.int32).at[ranking[jnp.where(places < fixed, places, passed)]].set(jnp.asarray(lengths, jnp.int32))

    lengths = jnp.where(number % 4 == 0, named(packed, number // 4), named(ordinary, number - number // 4 - 1))
    mixed = jax.random.permutation(jax.random.fold_in(own, 3), count)
    source_of, receiver = mixed[0:count // 2 * 2:2], mixed[1:count // 2 * 2:2]
    slack = jnp.minimum(lengths[source_of] - 1, reach - lengths[receiver]) // 2
    slack = jnp.where((source_of == ranking[0]) | (receiver == ranking[0]) | (lengths[receiver] == 0), 0, jnp.maximum(slack, 0))
    passed = jax.random.randint(jax.random.fold_in(own, 4), (count // 2,), 0, 1 << 20) % (slack + 1)
    lengths = lengths.at[source_of].add(-passed).at[receiver].add(passed)
    members = jnp.searchsorted(jnp.cumsum(lengths), jnp.arange(rows * top), side="right").astype(jnp.int32)
    grid = members.reshape(top, rows).T
    grid = grid[jax.random.permutation(jax.random.fold_in(own, 1), rows)]
    turn = jax.random.randint(jax.random.fold_in(own, 2), (rows, 1), 0, top)
    return jnp.take_along_axis(grid, (jnp.arange(top)[None, :] + turn) % top, axis=1)


def load_shares(count, total, most, skew, full):
    loads = [(1 << 20) // math.isqrt(rank ** skew) + 1 for rank in range(1, count + 1)]
    largest = most if full else min(most, max(-(-total // count), total * loads[0] // sum(loads)))
    least = 1 if total - largest >= count - 1 else 0
    holding, spare = [largest] + [least] * (count - 1), total - largest - least * (count - 1)
    while spare > 0:
        candidates = [i for i in range(1, count) if holding[i] < largest] or [i for i in range(1, count) if holding[i] < most]
        mass, remaining = sum([loads[i] for i in candidates]), spare
        for i in candidates:
            more = min(most - holding[i], max(1, remaining * loads[i] // mass), spare)
            holding[i] = holding[i] + more
            spare = spare - more
    return np.array(holding)


def noise(stream_key, dims, deviation, limit, split=(), kind=jnp.bfloat16):
    values = deviation * jax.random.normal(stream_key, dims, jnp.float32)
    if split:
        values = values * block_scale(stream_key, dims, split, -0.22, 0.18)
    return jnp.clip(values, -limit, limit).astype(kind)


def setup_inputs(seed: int = 0) -> dict:
    arg_keys = jax.random.split(jax.random.key(seed), 7)
    factor_rows = noise(arg_keys[0], (ROWS_TOTAL, K), 0.3, 2.0, ((0, 32),))
    factor_cols = noise(arg_keys[1], (COLS_TOTAL, K), 0.3, 2.0, ((0, 128),))
    observed = noise(arg_keys[2], (TILES, TB, TB), 1.0, 6.0, ((0, 128),))
    tile_row = place_ends(jax.random.randint(arg_keys[3], (TILES,), 0, RBD), jax.random.fold_in(arg_keys[3], 1), 0, RBD - 1).astype(jnp.int32)
    tile_owner_keys = jax.random.split(jax.random.fold_in(arg_keys[4], 1), TILES // TILES_DEV)
    tile_owner_turns = jax.random.permutation(jax.random.fold_in(arg_keys[4], 3), TILES // TILES_DEV)
    tile_owner = jax.vmap(lambda own, number: routed_block(jax.random.fold_in(arg_keys[4], 2), own, number, TILES_DEV, DEVICES, 1, CAP, 2))(tile_owner_keys, tile_owner_turns).reshape((TILES, 1))
    tile_sub = place_ends(jax.random.randint(arg_keys[5], (TILES,), 0, CBD), jax.random.fold_in(arg_keys[5], 1), 0, CBD - 1).astype(jnp.int32)
    return dict(factor_rows=factor_rows, factor_cols=factor_cols, observed=observed, tile_row=tile_row, tile_owner=tile_owner, tile_sub=tile_sub)


step_rate = 0.02
smooth_width = 0.5

def reference(factor_rows, factor_cols, observed, tile_row, tile_owner, tile_sub):
    row_blocks = factor_rows.reshape(N_ROWS * RBD, TB, K)
    col_blocks = factor_cols.reshape(DEVICES * CBD, TB, K)
    dev_row = jnp.arange(TILES, dtype=jnp.int32) // TILES_DEV // N_COLS
    row_ids = (dev_row * RBD + tile_row).astype(jnp.int32).reshape(DEVICES, TILES_DEV)
    col_ids = (tile_owner[:, 0] * CBD + tile_sub).astype(jnp.int32).reshape(DEVICES, TILES_DEV)
    observed_dev = observed.reshape(DEVICES, TILES_DEV, TB, TB)

    def per_device(totals, inputs_now):
        row_grad, col_grad = totals
        obs_now, row_now, col_now = inputs_now
        row_vals = row_blocks[row_now].astype(jnp.float32)
        col_vals = col_blocks[col_now].astype(jnp.float32)
        residual = jnp.einsum('tik,tjk->tij', row_vals, col_vals, precision=lax.Precision.HIGHEST) - obs_now.astype(jnp.float32)
        slopes = (residual / jnp.sqrt(residual * residual + smooth_width * smooth_width)).astype(jnp.bfloat16)
        slopes = lax.optimization_barrier(slopes).astype(jnp.float32)
        row_terms = jnp.einsum('tij,tjk->tik', slopes, col_vals, precision=lax.Precision.HIGHEST)
        col_terms = jnp.einsum('tij,tik->tjk', slopes, row_vals, precision=lax.Precision.HIGHEST).astype(jnp.bfloat16)
        col_terms = lax.optimization_barrier(col_terms).astype(jnp.float32)
        return ((row_grad.at[row_now].add(row_terms), col_grad.at[col_now].add(col_terms)), None)
    start = (jnp.zeros((N_ROWS * RBD, TB, K), jnp.float32), jnp.zeros((DEVICES * CBD, TB, K), jnp.float32))
    (row_grad, col_grad), unused = lax.scan(per_device, start, (observed_dev, row_ids, col_ids))
    rows_new = factor_rows.astype(jnp.float32) - step_rate * row_grad.reshape(ROWS_TOTAL, K)
    cols_new = factor_cols.astype(jnp.float32) - step_rate * col_grad.reshape(COLS_TOTAL, K)
    return (rows_new, cols_new)
```

```python
import functools

import jax
import jax.numpy as jnp
from jax import lax
from jax.experimental import pallas as pl
from jax.experimental.pallas import tpu as pltpu
from jax.sharding import PartitionSpec as P

MESH = pl.DeviceIdType.MESH
step_rate = 0.02
smooth_width = 0.5
SIDE = 4
CORES = 2
STEP_TILES = 4
SUM_SLOTS = 8


def position():
    rows = lax.axis_index("rows")
    return (
        lax.div(rows, SIDE * CORES),
        lax.rem(lax.div(rows, CORES), SIDE),
        lax.rem(rows, CORES),
        lax.axis_index("cols"),
    )


def device_at(y, x, core, z):
    return ((y * SIDE + x) * CORES + core, z)


AXES = (0, 1, 3)
ORDERS = ((0, 1, 3), (1, 3, 0), (3, 0, 1))


def gather_kernel(cuts, v_ref, o_ref, own_sem, send_sem, recv_sem, chip_send, chip_recv):
    me = position()

    def moved(axis, by):
        there = list(me)
        there[axis] = lax.rem(there[axis] + (by + SIDE), SIDE)
        return tuple(there)

    partner = (me[0], me[1], 1 - me[2], me[3])
    neighbours = [moved(axis, by) for axis in AXES for by in (1, -1)] + [partner]

    own = pltpu.make_async_copy(v_ref, o_ref.at[me], own_sem)
    own.start()
    barrier = pltpu.get_barrier_semaphore()
    for there in neighbours:
        pl.semaphore_signal(barrier, inc=1, device_id=device_at(*there), device_id_type=MESH)
    pl.semaphore_wait(barrier, len(neighbours))
    own.wait()

    def region(part, stage, by, half):
        order = ORDERS[part]
        low, size = cuts[part]
        where = list(me)
        for axis in order[:stage]:
            where[axis] = pl.ds(0, SIDE)
        where[order[stage]] = lax.rem(me[order[stage]] + (by + SIDE), SIDE)
        if half is not None:
            if stage == 0:
                first = size // 32 * 16
                low, size = (low, first) if half == 0 else (low + first, size - first)
            else:
                where[order[stage - 1]] = pl.ds(half * (SIDE // 2), SIDE // 2)
        return o_ref.at[tuple(where) + (pl.ds(low, size),)]

    def send(part, stage, step, way, by, half):
        block = region(part, stage, by, half)
        return pltpu.make_async_remote_copy(
            src_ref=block,
            dst_ref=block,
            send_sem=send_sem.at[part, stage, step, way],
            recv_sem=recv_sem.at[part, stage, step, way],
            device_id=device_at(*moved(ORDERS[part][stage], 1 if way == 0 else -1)),
            device_id_type=MESH,
        )

    def arrival(part, stage, step, way):
        by = (-1 if way == 0 else 1) * (step + 1)
        block = region(part, stage, by, None if step == 0 else way)
        return pltpu.make_async_remote_copy(
            src_ref=block,
            dst_ref=block,
            send_sem=send_sem.at[part, stage, step, way],
            recv_sem=recv_sem.at[part, stage, step, way],
            device_id=device_at(*moved(ORDERS[part][stage], 1 if way == 0 else -1)),
            device_id_type=MESH,
        )

    def across(part, piece, by):
        block = region(part, 2, by, None)
        return pltpu.make_async_remote_copy(
            src_ref=block,
            dst_ref=block,
            send_sem=chip_send.at[part, piece],
            recv_sem=chip_recv.at[part, piece],
            device_id=device_at(*partner),
            device_id_type=MESH,
        )

    def arrival_across(part, piece, by):
        where = [pl.ds(0, SIDE), pl.ds(0, SIDE), 1 - me[2], pl.ds(0, SIDE)]
        axis = ORDERS[part][2]
        where[axis] = lax.rem(me[axis] + (by + SIDE), SIDE)
        block = o_ref.at[tuple(where) + (pl.ds(*cuts[part]),)]
        return pltpu.make_async_remote_copy(
            src_ref=block,
            dst_ref=block,
            send_sem=chip_send.at[part, piece],
            recv_sem=chip_recv.at[part, piece],
            device_id=device_at(*partner),
            device_id_type=MESH,
        )

    started = []

    def begin(copy):
        copy.start()
        started.append(copy)

    parts = range(len(ORDERS))
    for stage in range(3):
        for part in parts:
            for way in (0, 1):
                begin(send(part, stage, 0, way, 0, None))
        if stage == 2:
            for part in parts:
                begin(across(part, 0, 0))
        for part in parts:
            for way in (0, 1):
                arrival(part, stage, 0, way).wait_recv()
                begin(send(part, stage, 1, way, -1 if way == 0 else 1, way))
        if stage == 2:
            for part in parts:
                begin(across(part, 1, -1))
                begin(across(part, 2, 1))
        for part in parts:
            for way in (0, 1):
                arrival(part, stage, 1, way).wait_recv()
            if stage == 2:
                begin(across(part, 3, 2))
    for part in parts:
        for piece, by in enumerate((0, -1, 1, 2)):
            arrival_across(part, piece, by).wait_recv()
    for copy in started:
        copy.wait_send()


def gather_all(shard):
    rows, rank = shard.shape
    third = rows // 48 * 16
    cuts = ((0, third + 16), (third + 16, third + 16), (2 * third + 32, rows - 2 * third - 32))
    return pl.pallas_call(
        functools.partial(gather_kernel, cuts),
        out_shape=jax.ShapeDtypeStruct((SIDE, SIDE, CORES, SIDE, rows, rank), shard.dtype),
        in_specs=[pl.BlockSpec(memory_space=pl.ANY)],
        out_specs=pl.BlockSpec(memory_space=pl.ANY),
        scratch_shapes=[
            pltpu.SemaphoreType.DMA,
            pltpu.SemaphoreType.DMA((3, 3, 2, 2)),
            pltpu.SemaphoreType.DMA((3, 3, 2, 2)),
            pltpu.SemaphoreType.DMA((3, 4)),
            pltpu.SemaphoreType.DMA((3, 4)),
        ],
        compiler_params=pltpu.CompilerParams(collective_id=0, has_side_effects=True),
    )(shard)


def tile_kernel(
    row_of, col_of, slot_of, u_ref, obs_ref, v_hbm, rows_ref, part_hbm, v_buf, part_buf, in_sem, out_sem
):
    step = pl.program_id(0)
    steps = pl.num_programs(0)
    now = lax.rem(step, 2)

    def fetch(at, slot, lane):
        return pltpu.make_async_copy(
            v_hbm.at[col_of[at * STEP_TILES + lane]], v_buf.at[slot, lane], in_sem.at[slot, lane]
        )

    def put(at, slot, lane):
        return pltpu.make_async_copy(
            part_buf.at[slot, lane], part_hbm.at[slot_of[at * STEP_TILES + lane]], out_sem.at[slot, lane]
        )

    @pl.when(step == 0)
    def _():
        rows_ref[...] = jnp.zeros_like(rows_ref)
        for lane in range(STEP_TILES):
            fetch(0, 0, lane).start()

    @pl.when(step + 1 < steps)
    def _():
        for lane in range(STEP_TILES):
            fetch(step + 1, 1 - now, lane).start()

    @pl.when(step >= 2)
    def _():
        for lane in range(STEP_TILES):
            put(step - 2, now, lane).wait()

    for lane in range(STEP_TILES):
        fetch(step, now, lane).wait()
    for lane in range(STEP_TILES):
        block = row_of[step * STEP_TILES + lane]
        u = u_ref[block]
        v = v_buf[now, lane]
        residual = lax.dot_general(
            u, v, (((1,), (1,)), ((), ())), preferred_element_type=jnp.float32
        ) - obs_ref[lane].astype(jnp.float32)
        slopes = (residual * lax.rsqrt(residual * residual + smooth_width * smooth_width)).astype(jnp.bfloat16)
        rows_ref[block] += jnp.dot(slopes, v, preferred_element_type=jnp.float32)
        part_buf[now, lane] = lax.dot_general(
            slopes, u, (((0,), (0,)), ((), ())), preferred_element_type=jnp.float32
        ).astype(jnp.bfloat16)
    for lane in range(STEP_TILES):
        put(step, now, lane).start()

    @pl.when(step + 1 == steps)
    def _():
        for lane in range(STEP_TILES):
            put(step - 1, 1 - now, lane).wait()
            put(step, now, lane).wait()


def tile_terms(row_of, col_of, slot_of, row_blocks, observed, col_blocks, slots):
    tiles, side, _ = observed.shape
    blocks, _, rank = row_blocks.shape
    return pl.pallas_call(
        tile_kernel,
        out_shape=(
            jax.ShapeDtypeStruct((blocks, side, rank), jnp.float32),
            jax.ShapeDtypeStruct((slots, side, rank), jnp.bfloat16),
        ),
        grid_spec=pltpu.PrefetchScalarGridSpec(
            num_scalar_prefetch=3,
            grid=(tiles // STEP_TILES,),
            in_specs=[
                pl.BlockSpec((blocks, side, rank), lambda i, *_: (0, 0, 0)),
                pl.BlockSpec((STEP_TILES, side, side), lambda i, *_: (i, 0, 0)),
                pl.BlockSpec(memory_space=pl.ANY),
            ],
            out_specs=(
                pl.BlockSpec((blocks, side, rank), lambda i, *_: (0, 0, 0)),
                pl.BlockSpec(memory_space=pl.ANY),
            ),
            scratch_shapes=[
                pltpu.VMEM((2, STEP_TILES, side, rank), jnp.bfloat16),
                pltpu.VMEM((2, STEP_TILES, side, rank), jnp.bfloat16),
                pltpu.SemaphoreType.DMA((2, STEP_TILES)),
                pltpu.SemaphoreType.DMA((2, STEP_TILES)),
            ],
        ),
        compiler_params=pltpu.CompilerParams(vmem_limit_bytes=32 << 20),
        cost_estimate=pl.CostEstimate(
            flops=6 * tiles * side * side * rank, bytes_accessed=4 * tiles * side * side, transcendentals=0
        ),
    )(row_of, col_of, slot_of, row_blocks, observed, col_blocks)


def sum_kernel(ids, factor_ref, back_ref, out_ref, total):
    step = pl.program_id(0)

    @pl.when(step == 0)
    def _():
        total[...] = jnp.zeros_like(total)

    for lane in range(SUM_SLOTS):
        block = ids[step * SUM_SLOTS + lane]

        @pl.when(block >= 0)
        def _():
            total[block] += back_ref[lane].astype(jnp.float32)

    @pl.when(step + 1 == pl.num_programs(0))
    def _():
        out_ref[...] = factor_ref[...].astype(jnp.float32) - step_rate * total[...]


def column_step(ids, factor, back):
    slots, side, rank = back.shape
    blocks = factor.shape[0]
    whole = pl.BlockSpec((blocks, side, rank), lambda i, *_: (0, 0, 0))
    return pl.pallas_call(
        sum_kernel,
        out_shape=jax.ShapeDtypeStruct((blocks, side, rank), jnp.float32),
        grid_spec=pltpu.PrefetchScalarGridSpec(
            num_scalar_prefetch=1,
            grid=(slots // SUM_SLOTS,),
            in_specs=[whole, pl.BlockSpec((SUM_SLOTS, side, rank), lambda i, *_: (i, 0, 0))],
            out_specs=whole,
            scratch_shapes=[pltpu.VMEM((blocks, side, rank), jnp.float32)],
        ),
        compiler_params=pltpu.CompilerParams(vmem_limit_bytes=32 << 20),
    )(ids, factor, back)


def body(factor_rows, factor_cols, observed, tile_row, tile_owner, tile_sub):
    tiles, side, _ = observed.shape
    rank = factor_rows.shape[1]
    peers = lax.axis_size(("rows", "cols"))
    me = lax.axis_index(("rows", "cols"))
    held = factor_cols.shape[0] // side
    owners = tile_owner[:, 0]
    codes = owners * held + tile_sub
    every = lax.all_gather(codes, ("rows", "cols"), axis=0, tiled=True).reshape(peers, tiles)

    order = jnp.arange(tiles, dtype=jnp.int32)
    repeat = jnp.any((owners[:, None] == owners[None, :]) & (order[None, :] < order[:, None]), axis=1)
    slot_of = owners * 2 + repeat.astype(jnp.int32)

    columns = gather_all(factor_cols).reshape(peers * held, side, rank)
    row_part, parts = tile_terms(
        tile_row,
        codes,
        slot_of,
        factor_rows.reshape(-1, side, rank),
        observed,
        columns,
        peers * 2,
    )
    back = lax.all_to_all(
        parts.reshape(peers, 2, side, rank), ("rows", "cols"), split_axis=0, concat_axis=0, tiled=True
    ).reshape(peers * 2, side, rank)

    mine = (every >= me * held) & (every < (me + 1) * held)
    first = jnp.min(jnp.where(mine, order[None, :], tiles), axis=1)
    last = jnp.max(jnp.where(mine, order[None, :], -1), axis=1)
    sub = every - me * held
    first_id = jnp.max(jnp.where(mine & (order[None, :] == first[:, None]), sub, -1), axis=1)
    last_id = jnp.max(
        jnp.where(mine & (order[None, :] == last[:, None]) & (last > first)[:, None], sub, -1), axis=1
    )
    ids = jnp.stack([first_id, last_id], axis=1).reshape(-1)

    cols_new = column_step(ids, factor_cols.reshape(held, side, rank), back).reshape(-1, rank)
    row_total = lax.psum(row_part.reshape(-1, rank), "cols")
    rows_new = factor_rows.astype(jnp.float32) - step_rate * row_total
    return (rows_new, cols_new)


def solution(mesh):
    return jax.shard_map(
        body,
        mesh=mesh,
        in_specs=(
            P("rows", None),
            P(("rows", "cols"), None),
            P(("rows", "cols"), None, None),
            P(("rows", "cols")),
            P(("rows", "cols"), None),
            P(("rows", "cols")),
        ),
        out_specs=(P("rows", None), P(("rows", "cols"), None)),
        check_vma=False,
    )
```

```python
import functools

import jax
import jax.numpy as jnp
from jax import lax
from jax.experimental import pallas as pl
from jax.experimental.pallas import tpu as pltpu
from jax.sharding import PartitionSpec as P

MESH = pl.DeviceIdType.MESH
step_rate = 0.02
smooth_width = 0.5
SIDE = 4
CORES = 2
STEP_TILES = 4
ROW_CUTS = ((0, 96), (96, 80), (176, 80))
BIN = 2 * SIDE * SIDE


def position():
    rows = lax.axis_index("rows")
    return (
        lax.div(rows, SIDE * CORES),
        lax.rem(lax.div(rows, CORES), SIDE),
        lax.rem(rows, CORES),
        lax.axis_index("cols"),
    )


def device_at(y, x, core, z):
    return ((y * SIDE + x) * CORES + core, z)


AXES = (0, 1, 3)
ORDERS = ((0, 1, 3), (1, 3, 0), (3, 0, 1))


def gather_kernel(cuts, v_ref, o_ref, own_sem, send_sem, recv_sem, chip_send, chip_recv):
    me = position()

    def moved(axis, by):
        there = list(me)
        there[axis] = lax.rem(there[axis] + (by + SIDE), SIDE)
        return tuple(there)

    partner = (me[0], me[1], 1 - me[2], me[3])
    neighbours = [moved(axis, by) for axis in AXES for by in (1, -1)] + [partner]

    own = pltpu.make_async_copy(v_ref, o_ref.at[me], own_sem)
    own.start()
    barrier = pltpu.get_barrier_semaphore()
    for there in neighbours:
        pl.semaphore_signal(barrier, inc=1, device_id=device_at(*there), device_id_type=MESH)
    pl.semaphore_wait(barrier, len(neighbours))
    own.wait()

    def region(part, stage, by, half):
        order = ORDERS[part]
        low, size = cuts[part]
        where = list(me)
        for axis in order[:stage]:
            where[axis] = pl.ds(0, SIDE)
        where[order[stage]] = lax.rem(me[order[stage]] + (by + SIDE), SIDE)
        if half is not None:
            if stage == 0:
                first = size // 32 * 16
                low, size = (low, first) if half == 0 else (low + first, size - first)
            else:
                where[order[stage - 1]] = pl.ds(half * (SIDE // 2), SIDE // 2)
        return o_ref.at[tuple(where) + (pl.ds(low, size),)]

    def send(part, stage, step, way, by, half):
        block = region(part, stage, by, half)
        return pltpu.make_async_remote_copy(
            src_ref=block,
            dst_ref=block,
            send_sem=send_sem.at[part, stage, step, way],
            recv_sem=recv_sem.at[part, stage, step, way],
            device_id=device_at(*moved(ORDERS[part][stage], 1 if way == 0 else -1)),
            device_id_type=MESH,
        )

    def arrival(part, stage, step, way):
        by = (-1 if way == 0 else 1) * (step + 1)
        block = region(part, stage, by, None if step == 0 else way)
        return pltpu.make_async_remote_copy(
            src_ref=block,
            dst_ref=block,
            send_sem=send_sem.at[part, stage, step, way],
            recv_sem=recv_sem.at[part, stage, step, way],
            device_id=device_at(*moved(ORDERS[part][stage], 1 if way == 0 else -1)),
            device_id_type=MESH,
        )

    def across(part, piece, by):
        block = region(part, 2, by, None)
        return pltpu.make_async_remote_copy(
            src_ref=block,
            dst_ref=block,
            send_sem=chip_send.at[part, piece],
            recv_sem=chip_recv.at[part, piece],
            device_id=device_at(*partner),
            device_id_type=MESH,
        )

    def arrival_across(part, piece, by):
        where = [pl.ds(0, SIDE), pl.ds(0, SIDE), 1 - me[2], pl.ds(0, SIDE)]
        axis = ORDERS[part][2]
        where[axis] = lax.rem(me[axis] + (by + SIDE), SIDE)
        block = o_ref.at[tuple(where) + (pl.ds(*cuts[part]),)]
        return pltpu.make_async_remote_copy(
            src_ref=block,
            dst_ref=block,
            send_sem=chip_send.at[part, piece],
            recv_sem=chip_recv.at[part, piece],
            device_id=device_at(*partner),
            device_id_type=MESH,
        )

    started = []

    def begin(copy):
        copy.start()
        started.append(copy)

    parts = range(len(ORDERS))
    for stage in range(3):
        for part in parts:
            for way in (0, 1):
                begin(send(part, stage, 0, way, 0, None))
        if stage == 2:
            for part in parts:
                begin(across(part, 0, 0))
        for part in parts:
            for way in (0, 1):
                arrival(part, stage, 0, way).wait_recv()
                begin(send(part, stage, 1, way, -1 if way == 0 else 1, way))
        if stage == 2:
            for part in parts:
                begin(across(part, 1, -1))
                begin(across(part, 2, 1))
        for part in parts:
            for way in (0, 1):
                arrival(part, stage, 1, way).wait_recv()
            if stage == 2:
                begin(across(part, 3, 2))
    for part in parts:
        for piece, by in enumerate((0, -1, 1, 2)):
            arrival_across(part, piece, by).wait_recv()
    for copy in started:
        copy.wait_send()


def gather_all(shard):
    rows, rank = shard.shape
    third = rows // 48 * 16
    cuts = ((0, third + 16), (third + 16, third + 16), (2 * third + 32, rows - 2 * third - 32))
    return pl.pallas_call(
        functools.partial(gather_kernel, cuts),
        out_shape=jax.ShapeDtypeStruct((SIDE, SIDE, CORES, SIDE, rows, rank), shard.dtype),
        in_specs=[pl.BlockSpec(memory_space=pltpu.HBM)],
        out_specs=pl.BlockSpec(memory_space=pltpu.HBM),
        scratch_shapes=[
            pltpu.SemaphoreType.DMA,
            pltpu.SemaphoreType.DMA((3, 3, 2, 2)),
            pltpu.SemaphoreType.DMA((3, 3, 2, 2)),
            pltpu.SemaphoreType.DMA((3, 4)),
            pltpu.SemaphoreType.DMA((3, 4)),
        ],
        compiler_params=pltpu.CompilerParams(collective_id=0, has_side_effects=True),
    )(shard)


def line_kernel(ids_ref, *refs):
    parts = len(ORDERS)
    sources, (ids_out, *targets) = refs[:parts], refs[parts : 2 * parts + 1]
    own_sem, send_sem, recv_sem, ids_send, ids_recv = refs[2 * parts + 1 :]
    me = position()
    offsets = ((2, 0), (1, 0), (3, 0), (2, 1), (1, 1), (3, 1), (0, 1))

    def moved(part, by, flip):
        there = list(me)
        axis = ORDERS[part][0]
        there[axis] = lax.rem(there[axis] + by, SIDE)
        there[2] = 1 - me[2] if flip else me[2]
        return tuple(there)

    def bin_of(part, there):
        return there[ORDERS[part][0]] * CORES + there[2]

    def slots(at):
        return pl.ds(pl.multiple_of(at * BIN, BIN), BIN)

    copies = []
    for part in range(parts):
        here = bin_of(part, me)
        copies.append(
            pltpu.make_async_copy(
                sources[part].at[slots(here)], targets[part].at[slots(here)], own_sem.at[part, 0]
            )
        )
        line = part * CORES * SIDE
        copies.append(
            pltpu.make_async_copy(ids_ref.at[line + here], ids_out.at[line + here], own_sem.at[part, 1])
        )
    for copy in copies:
        copy.start()

    greeted = [moved(part, *offset) for part in range(parts) for offset in offsets[:-1]]
    greeted.append(moved(0, 0, 1))
    barrier = pltpu.get_barrier_semaphore()
    for there in greeted:
        pl.semaphore_signal(barrier, inc=1, device_id=device_at(*there), device_id_type=MESH)
    pl.semaphore_wait(barrier, len(greeted))

    def trade(part, place, start):
        by, flip = offsets[place]
        to, source = moved(part, by, flip), moved(part, SIDE - by if by else 0, flip)
        line = part * CORES * SIDE
        filled = bin_of(part, me) if start else bin_of(part, source)
        taken = bin_of(part, to)
        return (
            pltpu.make_async_remote_copy(
                src_ref=sources[part].at[slots(taken)],
                dst_ref=targets[part].at[slots(filled)],
                send_sem=send_sem.at[part, place],
                recv_sem=recv_sem.at[part, place],
                device_id=device_at(*to),
                device_id_type=MESH,
            ),
            pltpu.make_async_remote_copy(
                src_ref=ids_ref.at[line + taken],
                dst_ref=ids_out.at[line + filled],
                send_sem=ids_send.at[part, place],
                recv_sem=ids_recv.at[part, place],
                device_id=device_at(*to),
                device_id_type=MESH,
            ),
        )

    for place in range(len(offsets)):
        for part in range(parts):
            for copy in trade(part, place, True):
                copy.start()
    for place in range(len(offsets)):
        for part in range(parts):
            for copy in trade(part, place, False):
                copy.wait_recv()
            for copy in trade(part, place, True):
                copy.wait_send()
    for copy in copies:
        copy.wait()


def line_exchange(ids, sources):
    spec = pl.BlockSpec(memory_space=pltpu.HBM)
    parts = len(sources)
    return pl.pallas_call(
        line_kernel,
        out_shape=tuple(jax.ShapeDtypeStruct(a.shape, a.dtype) for a in (ids, *sources)),
        in_specs=[spec] * (parts + 1),
        out_specs=(spec,) * (parts + 1),
        scratch_shapes=[pltpu.SemaphoreType.DMA((parts, 2))] + [pltpu.SemaphoreType.DMA((parts, 7))] * 4,
        compiler_params=pltpu.CompilerParams(collective_id=1, has_side_effects=True),
    )(ids, *sources)


def plane_kernel(*refs):
    parts = len(ORDERS)
    sources, targets, between = refs[:parts], refs[parts : 2 * parts], refs[2 * parts : 3 * parts]
    own_sem, late_sem, first_send, first_recv, then_send, then_recv = refs[3 * parts :]
    me = position()
    hops = (2, 1, 3)

    def moved(axis, by):
        there = list(me)
        there[axis] = lax.rem(there[axis] + by, SIDE)
        return tuple(there)

    own = []
    for part in range(parts):
        at = me[ORDERS[part][1]]
        own.append(pltpu.make_async_copy(sources[part].at[at], between[part].at[at], own_sem.at[part]))
    for copy in own:
        copy.start()

    greeted = [moved(axis, by) for axis in AXES for by in hops]
    barrier = pltpu.get_barrier_semaphore()
    for there in greeted:
        pl.semaphore_signal(barrier, inc=1, device_id=device_at(*there), device_id_type=MESH)
    pl.semaphore_wait(barrier, len(greeted))

    def first(part, hop, turn, start):
        _, axis, last = ORDERS[part]
        by = hops[hop]
        to = moved(axis, by)
        filled = me[axis] if start else moved(axis, SIDE - by)[axis]
        row = lax.rem(me[last] + turn, SIDE)
        return pltpu.make_async_remote_copy(
            src_ref=sources[part].at[to[axis], row],
            dst_ref=between[part].at[filled, row],
            send_sem=first_send.at[part, hop, turn],
            recv_sem=first_recv.at[part, hop, turn],
            device_id=device_at(*to),
            device_id_type=MESH,
        )

    def then(part, hop, start):
        last = ORDERS[part][2]
        by = hops[hop]
        to = moved(last, by)
        filled = me[last] if start else moved(last, SIDE - by)[last]
        return pltpu.make_async_remote_copy(
            src_ref=between[part].at[:, to[last]],
            dst_ref=targets[part].at[:, filled],
            send_sem=then_send.at[part, hop],
            recv_sem=then_recv.at[part, hop],
            device_id=device_at(*to),
            device_id_type=MESH,
        )

    turns = hops + (0,)
    for turn in turns:
        for hop in range(len(hops)):
            for part in range(parts):
                first(part, hop, turn, True).start()
    for copy in own:
        copy.wait()
    for place, turn in enumerate(turns):
        for part in range(parts):
            for hop in range(len(hops)):
                first(part, hop, turn, False).wait_recv()
            if turn:
                then(part, place, True).start()
    late = []
    for part in range(parts):
        at = me[ORDERS[part][2]]
        late.append(
            pltpu.make_async_copy(between[part].at[:, at], targets[part].at[:, at], late_sem.at[part])
        )
    for copy in late:
        copy.start()
    for part in range(parts):
        for hop in range(len(hops)):
            then(part, hop, False).wait_recv()
            then(part, hop, True).wait_send()
            for turn in turns:
                first(part, hop, turn, True).wait_send()
    for copy in late:
        copy.wait()


def plane_exchange(sums):
    spec = pl.BlockSpec(memory_space=pltpu.HBM)
    parts = len(sums)
    shapes = tuple(jax.ShapeDtypeStruct(a.shape, a.dtype) for a in sums)
    return pl.pallas_call(
        plane_kernel,
        out_shape=shapes * 2,
        in_specs=[spec] * parts,
        out_specs=(spec,) * (2 * parts),
        scratch_shapes=[
            pltpu.SemaphoreType.DMA((parts,)),
            pltpu.SemaphoreType.DMA((parts,)),
            pltpu.SemaphoreType.DMA((parts, 3, SIDE)),
            pltpu.SemaphoreType.DMA((parts, 3, SIDE)),
            pltpu.SemaphoreType.DMA((parts, 3)),
            pltpu.SemaphoreType.DMA((parts, 3)),
        ],
        compiler_params=pltpu.CompilerParams(collective_id=2, has_side_effects=True),
    )(*sums)[:parts]


def tile_kernel(row_of, col_of, slot_of, u_ref, obs_ref, v_hbm, rows_ref, *refs):
    parts = len(ROW_CUTS)
    part_hbm, (v_buf, part_buf, in_sem, out_sem) = refs[:parts], refs[parts:]
    step = pl.program_id(0)
    steps = pl.num_programs(0)
    now = lax.rem(step, 2)
    tiles = steps * STEP_TILES

    def fetch(at, slot, lane):
        return pltpu.make_async_copy(
            v_hbm.at[col_of[at * STEP_TILES + lane]], v_buf.at[slot, lane], in_sem.at[slot, lane]
        )

    def put(at, slot, lane):
        return [
            pltpu.make_async_copy(
                part_buf.at[slot, lane, pl.ds(*cut)],
                part_hbm[part].at[slot_of[part * tiles + at * STEP_TILES + lane]],
                out_sem.at[part, slot, lane],
            )
            for part, cut in enumerate(ROW_CUTS)
        ]

    @pl.when(step == 0)
    def _():
        rows_ref[...] = jnp.zeros_like(rows_ref)
        for lane in range(STEP_TILES):
            fetch(0, 0, lane).start()

    @pl.when(step + 1 < steps)
    def _():
        for lane in range(STEP_TILES):
            fetch(step + 1, 1 - now, lane).start()

    @pl.when(step >= 2)
    def _():
        for lane in range(STEP_TILES):
            for copy in put(step - 2, now, lane):
                copy.wait()

    for lane in range(STEP_TILES):
        fetch(step, now, lane).wait()
    for lane in range(STEP_TILES):
        block = row_of[step * STEP_TILES + lane]
        u = u_ref[block]
        v = v_buf[now, lane]
        residual = lax.dot_general(
            u, v, (((1,), (1,)), ((), ())), preferred_element_type=jnp.float32
        ) - obs_ref[lane].astype(jnp.float32)
        slopes = (residual * lax.rsqrt(residual * residual + smooth_width * smooth_width)).astype(jnp.bfloat16)
        rows_ref[block] += jnp.dot(slopes, v, preferred_element_type=jnp.float32)
        part_buf[now, lane] = lax.dot_general(
            slopes, u, (((0,), (0,)), ((), ())), preferred_element_type=jnp.float32
        ).astype(jnp.bfloat16)
    for lane in range(STEP_TILES):
        for copy in put(step, now, lane):
            copy.start()

    @pl.when(step + 1 == steps)
    def _():
        for lane in range(STEP_TILES):
            for copy in put(step - 1, 1 - now, lane) + put(step, now, lane):
                copy.wait()


def tile_terms(row_of, col_of, slot_of, row_blocks, observed, col_blocks, slots):
    tiles, side, _ = observed.shape
    blocks, _, rank = row_blocks.shape
    parts = len(ROW_CUTS)
    hbm = pl.BlockSpec(memory_space=pltpu.HBM)
    return pl.pallas_call(
        tile_kernel,
        out_shape=(
            jax.ShapeDtypeStruct((blocks, side, rank), jnp.float32),
            *(jax.ShapeDtypeStruct((slots, size, rank), jnp.bfloat16) for _, size in ROW_CUTS),
        ),
        grid_spec=pltpu.PrefetchScalarGridSpec(
            num_scalar_prefetch=3,
            grid=(tiles // STEP_TILES,),
            in_specs=[
                pl.BlockSpec((blocks, side, rank), lambda i, *_: (0, 0, 0)),
                pl.BlockSpec((STEP_TILES, side, side), lambda i, *_: (i, 0, 0)),
                hbm,
            ],
            out_specs=(pl.BlockSpec((blocks, side, rank), lambda i, *_: (0, 0, 0)),) + (hbm,) * parts,
            scratch_shapes=[
                pltpu.VMEM((2, STEP_TILES, side, rank), jnp.bfloat16),
                pltpu.VMEM((2, STEP_TILES, side, rank), jnp.bfloat16),
                pltpu.SemaphoreType.DMA((2, STEP_TILES)),
                pltpu.SemaphoreType.DMA((parts, 2, STEP_TILES)),
            ],
        ),
        compiler_params=pltpu.CompilerParams(vmem_limit_bytes=60 << 20),
        cost_estimate=pl.CostEstimate(
            flops=6 * tiles * side * side * rank, bytes_accessed=4 * tiles * side * side, transcendentals=0
        ),
    )(row_of, col_of, slot_of, row_blocks, observed, col_blocks)


def block_kernel(ids, *refs):
    parts = len(ROW_CUTS)
    sources, targets, totals = refs[:parts], refs[parts : 2 * parts], refs[2 * parts :]
    step = pl.program_id(0)
    bins = pl.num_programs(0)

    @pl.when(step == 0)
    def _():
        for total in totals:
            total[...] = jnp.zeros_like(total)

    def add(lane, carry):
        for part in range(parts):
            block = ids[(part * bins + step) * 128 + lane]

            @pl.when(block >= 0)
            def _(part=part, block=block):
                totals[part][block] += sources[part][lane].astype(jnp.float32)

        return carry

    lax.fori_loop(0, BIN, add, 0)

    @pl.when(step + 1 == bins)
    def _():
        for part in range(parts):
            targets[part][...] = totals[part][...].astype(jnp.bfloat16)


def block_sums(ids, sources, blocks):
    rank = sources[0].shape[-1]
    whole = tuple((blocks, size, rank) for _, size in ROW_CUTS)
    return pl.pallas_call(
        block_kernel,
        out_shape=tuple(jax.ShapeDtypeStruct(shape, jnp.bfloat16) for shape in whole),
        grid_spec=pltpu.PrefetchScalarGridSpec(
            num_scalar_prefetch=1,
            grid=(sources[0].shape[0] // BIN,),
            in_specs=[pl.BlockSpec((BIN, size, rank), lambda i, *_: (i, 0, 0)) for _, size in ROW_CUTS],
            out_specs=tuple(
                pl.BlockSpec(shape, lambda i, *_: (0, 0, 0), pipeline_mode=pl.Buffered(1)) for shape in whole
            ),
            scratch_shapes=[pltpu.VMEM(shape, jnp.float32) for shape in whole],
        ),
        compiler_params=pltpu.CompilerParams(vmem_limit_bytes=60 << 20),
    )(ids, *sources)


def column_kernel(factor_ref, *refs):
    *sources, out_ref = refs
    for (low, size), source in zip(ROW_CUTS, sources):
        rows = pl.ds(low, size)
        total = source[0, 0].astype(jnp.float32)
        for sender in range(1, source.shape[0]):
            total += source[sender, 0].astype(jnp.float32)
        out_ref[0, rows] = factor_ref[0, rows].astype(jnp.float32) - step_rate * total


def column_step(factor, sums):
    held, side, rank = factor.shape
    block = pl.BlockSpec((1, side, rank), lambda i: (i, 0, 0))
    return pl.pallas_call(
        column_kernel,
        out_shape=jax.ShapeDtypeStruct(factor.shape, jnp.float32),
        grid=(held,),
        in_specs=[block]
        + [pl.BlockSpec((SIDE * SIDE, 1, size, rank), lambda i: (0, i, 0, 0)) for _, size in ROW_CUTS],
        out_specs=block,
        compiler_params=pltpu.CompilerParams(vmem_limit_bytes=60 << 20),
    )(factor, *sums)


def body(factor_rows, factor_cols, observed, tile_row, tile_owner, tile_sub):
    tiles, side, _ = observed.shape
    rank = factor_rows.shape[1]
    peers = lax.axis_size(("rows", "cols"))
    held = factor_cols.shape[0] // side
    owners = tile_owner[:, 0]
    codes = owners * held + tile_sub
    spots = {
        0: owners // (SIDE * SIDE * CORES),
        1: owners // (SIDE * CORES) % SIDE,
        2: owners // SIDE % CORES,
        3: owners % SIDE,
    }
    bins = jnp.stack([spots[first] * CORES + spots[2] for first, _, _ in ORDERS])
    blocks = jnp.stack([(spots[second] * SIDE + spots[third]) * held + tile_sub for _, second, third in ORDERS])
    order = jnp.arange(tiles, dtype=jnp.int32)
    earlier = (bins[:, :, None] == bins[:, None, :]) & (order[None, None, :] < order[None, :, None])
    slot_of = bins * BIN + jnp.sum(earlier.astype(jnp.int32), axis=2)
    slots = CORES * SIDE * BIN
    place = jnp.arange(slots, dtype=jnp.int32)
    ids = jnp.max(
        jnp.where(slot_of[:, None, :] == place[None, :, None], blocks[:, None, :], -1), axis=2
    ).reshape(len(ORDERS) * CORES * SIDE, 1, BIN)
    ids = jnp.pad(ids, ((0, 0), (0, 0), (0, 128 - BIN)), constant_values=-1)

    columns = gather_all(factor_cols).reshape(peers * held, side, rank)
    row_part, *parts = tile_terms(
        tile_row,
        codes,
        slot_of.reshape(-1),
        factor_rows.reshape(-1, side, rank),
        observed,
        columns,
        slots,
    )
    row_total = lax.psum(row_part.reshape(-1, rank), "cols")
    ids_here, *parts_here = line_exchange(ids, parts)
    sums = block_sums(ids_here.reshape(-1), parts_here, SIDE * SIDE * held)
    sums = plane_exchange([a.reshape(SIDE, SIDE, held, *a.shape[1:]) for a in sums])
    cols_new = column_step(
        factor_cols.reshape(held, side, rank), [a.reshape(SIDE * SIDE, *a.shape[2:]) for a in sums]
    ).reshape(-1, rank)
    rows_new = factor_rows.astype(jnp.float32) - step_rate * row_total
    return (rows_new, cols_new)


def solution(mesh):
    return jax.shard_map(
        body,
        mesh=mesh,
        in_specs=(
            P("rows", None),
            P(("rows", "cols"), None),
            P(("rows", "cols"), None, None),
            P(("rows", "cols")),
            P(("rows", "cols"), None),
            P(("rows", "cols")),
        ),
        out_specs=(P("rows", None), P(("rows", "cols"), None)),
        check_vma=False,
    )
```

```python
import functools

import jax
import jax.numpy as jnp
from jax import lax
from jax.experimental import pallas as pl
from jax.experimental.pallas import tpu as pltpu
from jax.sharding import PartitionSpec as P

MESH = pl.DeviceIdType.MESH
step_rate = 0.02
smooth_width = 0.5
SIDE = 4
CORES = 2
STEP_TILES = 4
ROW_CUTS = ((0, 96), (96, 80), (176, 80))
BIN = 2 * SIDE * SIDE


def position():
    rows = lax.axis_index("rows")
    return (
        lax.div(rows, SIDE * CORES),
        lax.rem(lax.div(rows, CORES), SIDE),
        lax.rem(rows, CORES),
        lax.axis_index("cols"),
    )


def device_at(y, x, core, z):
    return ((y * SIDE + x) * CORES + core, z)


AXES = (0, 1, 3)
ORDERS = ((0, 1, 3), (1, 3, 0), (3, 0, 1))


def gather_kernel(
    cuts, v_ref, o_ref, held, own_sem, send_sem, recv_sem, slab_send, slab_recv, chip_send, chip_recv
):
    me = position()

    def moved(axis, by):
        there = list(me)
        there[axis] = lax.rem(there[axis] + (by + SIDE), SIDE)
        return tuple(there)

    partner = (me[0], me[1], 1 - me[2], me[3])
    neighbours = [moved(axis, by) for axis in AXES for by in (1, -1)] + [partner]

    load = pltpu.make_async_copy(v_ref, held, own_sem.at[0])
    load.start()
    barrier = pltpu.get_barrier_semaphore()
    for there in neighbours:
        pl.semaphore_signal(barrier, inc=1, device_id=device_at(*there), device_id_type=MESH)
    pl.semaphore_wait(barrier, len(neighbours))
    load.wait()
    own = pltpu.make_async_copy(held, o_ref.at[me], own_sem.at[1])
    own.start()

    def region(part, stage, by, half):
        order = ORDERS[part]
        low, size = cuts[part]
        where = list(me)
        for axis in order[:stage]:
            where[axis] = pl.ds(0, SIDE)
        where[order[stage]] = lax.rem(me[order[stage]] + (by + SIDE), SIDE)
        if half is not None:
            if stage == 0:
                first = size // 32 * 16
                low, size = (low, first) if half == 0 else (low + first, size - first)
            else:
                where[order[stage - 1]] = pl.ds(half * (SIDE // 2), SIDE // 2)
        return o_ref.at[tuple(where) + (pl.ds(low, size),)]

    def send(part, stage, step, way, by, half):
        block = region(part, stage, by, half)
        return pltpu.make_async_remote_copy(
            src_ref=held.at[pl.ds(*cuts[part])] if stage == step == 0 else block,
            dst_ref=block,
            send_sem=send_sem.at[part, stage, step, way],
            recv_sem=recv_sem.at[part, stage, step, way],
            device_id=device_at(*moved(ORDERS[part][stage], 1 if way == 0 else -1)),
            device_id_type=MESH,
        )

    def arrival(part, stage, step, way):
        by = (-1 if way == 0 else 1) * (step + 1)
        block = region(part, stage, by, None if step == 0 else way)
        return pltpu.make_async_remote_copy(
            src_ref=block,
            dst_ref=block,
            send_sem=send_sem.at[part, stage, step, way],
            recv_sem=recv_sem.at[part, stage, step, way],
            device_id=device_at(*moved(ORDERS[part][stage], 1 if way == 0 else -1)),
            device_id_type=MESH,
        )

    def slab(part, core, by, place):
        order = ORDERS[part]
        where = list(me)
        where[2] = core
        where[order[0]] = pl.ds(0, SIDE)
        where[order[1]] = place
        where[order[2]] = lax.rem(me[order[2]] + (by + SIDE), SIDE)
        return o_ref.at[tuple(where) + (pl.ds(*cuts[part]),)]

    def pass_on(part, place, way, by):
        block = slab(part, me[2], by, place)
        return pltpu.make_async_remote_copy(
            src_ref=block,
            dst_ref=block,
            send_sem=slab_send.at[part, place, way, abs(by)],
            recv_sem=slab_recv.at[part, place, way, abs(by)],
            device_id=device_at(*moved(ORDERS[part][2], 1 if way == 0 else -1)),
            device_id_type=MESH,
        )

    def passed(part, place, way, step):
        block = slab(part, me[2], (-1 if way == 0 else 1) * (step + 1), place)
        return pltpu.make_async_remote_copy(
            src_ref=block,
            dst_ref=block,
            send_sem=slab_send.at[part, place, way, step],
            recv_sem=slab_recv.at[part, place, way, step],
            device_id=device_at(*moved(ORDERS[part][2], 1 if way == 0 else -1)),
            device_id_type=MESH,
        )

    def across(part, place, piece, core):
        block = slab(part, core, (0, -1, 1, 2)[piece], place)
        return pltpu.make_async_remote_copy(
            src_ref=block,
            dst_ref=block,
            send_sem=chip_send.at[part, place, piece],
            recv_sem=chip_recv.at[part, place, piece],
            device_id=device_at(*partner),
            device_id_type=MESH,
        )

    started = []

    def begin(copy):
        copy.start()
        started.append(copy)

    parts = range(len(ORDERS))
    for stage in range(2):
        for part in parts:
            for way in (0, 1):
                begin(send(part, stage, 0, way, 0, None))
        for part in parts:
            for way in (0, 1):
                arrival(part, stage, 0, way).wait_recv()
                begin(send(part, stage, 1, way, -1 if way == 0 else 1, way))
        for part in parts:
            for way in (0, 1):
                arrival(part, stage, 1, way).wait_recv()
        if stage == 0:
            own.wait()
    forwarder = {0: 0, 2: 0, 1: 1, 3: 1}
    places = (0, 1, 2, 3)
    for place in places:
        for part in parts:
            for way in (0, 1):
                begin(pass_on(part, place, way, 0))
        for part in parts:
            begin(across(part, place, 0, me[2]))
    for place in places:
        for part in parts:
            for way in (0, 1):
                passed(part, place, way, 0).wait_recv()
                if forwarder[place] == way:
                    begin(pass_on(part, place, way, -1 if way == 0 else 1))
                begin(across(part, place, 1 + way, me[2]))
    for place in places:
        for part in parts:
            passed(part, place, forwarder[place], 1).wait_recv()
            begin(across(part, place, 3, me[2]))
    for place in places:
        for part in parts:
            for piece in range(4):
                across(part, place, piece, 1 - me[2]).wait_recv()
    for copy in started:
        copy.wait_send()


def gather_all(shard):
    rows, rank = shard.shape
    third = rows // 48 * 16
    cuts = ((0, third + 16), (third + 16, third + 16), (2 * third + 32, rows - 2 * third - 32))
    return pl.pallas_call(
        functools.partial(gather_kernel, cuts),
        out_shape=jax.ShapeDtypeStruct((SIDE, SIDE, CORES, SIDE, rows, rank), shard.dtype),
        in_specs=[pl.BlockSpec(memory_space=pltpu.HBM)],
        out_specs=pl.BlockSpec(memory_space=pltpu.HBM),
        scratch_shapes=[
            pltpu.VMEM((rows, rank), shard.dtype),
            pltpu.SemaphoreType.DMA((2,)),
            pltpu.SemaphoreType.DMA((3, 2, 2, 2)),
            pltpu.SemaphoreType.DMA((3, 2, 2, 2)),
            pltpu.SemaphoreType.DMA((3, 4, 2, 2)),
            pltpu.SemaphoreType.DMA((3, 4, 2, 2)),
            pltpu.SemaphoreType.DMA((3, 4, 4)),
            pltpu.SemaphoreType.DMA((3, 4, 4)),
        ],
        compiler_params=pltpu.CompilerParams(collective_id=0, has_side_effects=True),
    )(shard)


def line_kernel(ids_ref, *refs):
    parts = len(ORDERS)
    sources, (ids_out, *targets) = refs[:parts], refs[parts : 2 * parts + 1]
    held = refs[2 * parts + 1 : 3 * parts + 2]
    own_sem, send_sem, recv_sem, ids_send, ids_recv = refs[3 * parts + 2 :]
    me = position()
    offsets = ((1, 0), (3, 0), (2, 0), (1, 1), (3, 1), (2, 1), (0, 1))

    def moved(part, by, flip):
        there = list(me)
        axis = ORDERS[part][0]
        there[axis] = lax.rem(there[axis] + by, SIDE)
        there[2] = 1 - me[2] if flip else me[2]
        return tuple(there)

    def bin_of(part, there):
        return there[ORDERS[part][0]] * CORES + there[2]

    def slots(at):
        return pl.ds(pl.multiple_of(at * BIN, BIN), BIN)

    loads, copies = [], []
    for part in range(parts):
        here = bin_of(part, me)
        line = part * CORES * SIDE + here
        loads.append(pltpu.make_async_copy(sources[part].at[slots(here)], held[part], own_sem.at[part, 0]))
        loads.append(pltpu.make_async_copy(ids_ref.at[line], held[parts].at[part], own_sem.at[part, 1]))
        copies.append(pltpu.make_async_copy(held[part], targets[part].at[slots(here)], own_sem.at[part, 2]))
        copies.append(pltpu.make_async_copy(held[parts].at[part], ids_out.at[line], own_sem.at[part, 3]))
    for copy in loads:
        copy.start()

    greeted = [moved(part, *offset) for part in range(parts) for offset in offsets[:-1]]
    greeted.append(moved(0, 0, 1))
    barrier = pltpu.get_barrier_semaphore()
    for there in greeted:
        pl.semaphore_signal(barrier, inc=1, device_id=device_at(*there), device_id_type=MESH)
    pl.semaphore_wait(barrier, len(greeted))

    def trade(part, place, start):
        by, flip = offsets[place]
        to, source = moved(part, by, flip), moved(part, SIDE - by if by else 0, flip)
        line = part * CORES * SIDE
        filled = bin_of(part, me) if start else bin_of(part, source)
        taken = bin_of(part, to)
        return (
            pltpu.make_async_remote_copy(
                src_ref=sources[part].at[slots(taken)],
                dst_ref=targets[part].at[slots(filled)],
                send_sem=send_sem.at[part, place],
                recv_sem=recv_sem.at[part, place],
                device_id=device_at(*to),
                device_id_type=MESH,
            ),
            pltpu.make_async_remote_copy(
                src_ref=ids_ref.at[line + taken],
                dst_ref=ids_out.at[line + filled],
                send_sem=ids_send.at[part, place],
                recv_sem=ids_recv.at[part, place],
                device_id=device_at(*to),
                device_id_type=MESH,
            ),
        )

    for places in ((0, 1), (2,), (6,), (3, 4), (5,)):
        for part in range(parts):
            for place in places:
                for copy in trade(part, place, True):
                    copy.start()
    for load, copy in zip(loads, copies):
        load.wait()
        copy.start()
    for place in range(len(offsets)):
        for part in range(parts):
            for copy in trade(part, place, False):
                copy.wait_recv()
            for copy in trade(part, place, True):
                copy.wait_send()
    for copy in copies:
        copy.wait()


def line_exchange(ids, sources):
    spec = pl.BlockSpec(memory_space=pltpu.HBM)
    parts = len(sources)
    return pl.pallas_call(
        line_kernel,
        out_shape=tuple(jax.ShapeDtypeStruct(a.shape, a.dtype) for a in (ids, *sources)),
        in_specs=[spec] * (parts + 1),
        out_specs=(spec,) * (parts + 1),
        scratch_shapes=[pltpu.VMEM((BIN, *a.shape[1:]), a.dtype) for a in sources]
        + [pltpu.VMEM((parts, *ids.shape[1:]), ids.dtype), pltpu.SemaphoreType.DMA((parts, 4))]
        + [pltpu.SemaphoreType.DMA((parts, 7))] * 4,
        compiler_params=pltpu.CompilerParams(collective_id=1, has_side_effects=True),
    )(ids, *sources)


def plane_kernel(*refs):
    parts = len(ORDERS)
    sources, targets, between = refs[:parts], refs[parts : 2 * parts], refs[2 * parts : 3 * parts]
    held, late_held = refs[3 * parts : 4 * parts], refs[4 * parts : 5 * parts]
    own_sem, late_sem, first_send, first_recv, then_send, then_recv = refs[5 * parts :]
    me = position()
    hops = (1, 3, 2)

    def moved(axis, by):
        there = list(me)
        there[axis] = lax.rem(there[axis] + by, SIDE)
        return tuple(there)

    loads, own = [], []
    for part in range(parts):
        at = me[ORDERS[part][1]]
        loads.append(pltpu.make_async_copy(sources[part].at[at], held[part], own_sem.at[part, 0]))
        own.append(pltpu.make_async_copy(held[part], between[part].at[at], own_sem.at[part, 1]))
    for copy in loads:
        copy.start()

    greeted = [moved(axis, by) for axis in AXES for by in hops]
    barrier = pltpu.get_barrier_semaphore()
    for there in greeted:
        pl.semaphore_signal(barrier, inc=1, device_id=device_at(*there), device_id_type=MESH)
    pl.semaphore_wait(barrier, len(greeted))

    def first(part, hop, turn, start):
        _, axis, last = ORDERS[part]
        by = hops[hop]
        to = moved(axis, by)
        filled = me[axis] if start else moved(axis, SIDE - by)[axis]
        row = lax.rem(me[last] + turn, SIDE)
        return pltpu.make_async_remote_copy(
            src_ref=sources[part].at[to[axis], row],
            dst_ref=between[part].at[filled, row],
            send_sem=first_send.at[part, hop, turn],
            recv_sem=first_recv.at[part, hop, turn],
            device_id=device_at(*to),
            device_id_type=MESH,
        )

    def then(part, hop, start):
        last = ORDERS[part][2]
        by = hops[hop]
        to = moved(last, by)
        filled = me[last] if start else moved(last, SIDE - by)[last]
        return pltpu.make_async_remote_copy(
            src_ref=between[part].at[:, to[last]],
            dst_ref=targets[part].at[:, filled],
            send_sem=then_send.at[part, hop],
            recv_sem=then_recv.at[part, hop],
            device_id=device_at(*to),
            device_id_type=MESH,
        )

    turns = hops + (0,)
    for turn in turns:
        for places in ((0, 1), (2,)):
            for part in range(parts):
                for hop in places:
                    first(part, hop, turn, True).start()
    for load, copy in zip(loads, own):
        load.wait()
        copy.start()
    for copy in own:
        copy.wait()
    for place, turn in enumerate(turns):
        for part in range(parts):
            for hop in range(len(hops)):
                first(part, hop, turn, False).wait_recv()
            if turn:
                then(part, place, True).start()
    late = []
    for part in range(parts):
        at = me[ORDERS[part][2]]
        load = pltpu.make_async_copy(between[part].at[:, at], late_held[part], late_sem.at[part, 0])
        load.start()
        copy = pltpu.make_async_copy(late_held[part], targets[part].at[:, at], late_sem.at[part, 1])
        late.append((load, copy))
    for load, copy in late:
        load.wait()
        copy.start()
    for part in range(parts):
        for hop in range(len(hops)):
            then(part, hop, False).wait_recv()
            then(part, hop, True).wait_send()
            for turn in turns:
                first(part, hop, turn, True).wait_send()
    for _, copy in late:
        copy.wait()


def plane_exchange(sums):
    spec = pl.BlockSpec(memory_space=pltpu.HBM)
    parts = len(sums)
    shapes = tuple(jax.ShapeDtypeStruct(a.shape, a.dtype) for a in sums)
    return pl.pallas_call(
        plane_kernel,
        out_shape=shapes * 2,
        in_specs=[spec] * parts,
        out_specs=(spec,) * (2 * parts),
        scratch_shapes=[pltpu.VMEM(a.shape[1:], a.dtype) for a in sums] * 2
        + [
            pltpu.SemaphoreType.DMA((parts, 2)),
            pltpu.SemaphoreType.DMA((parts, 2)),
            pltpu.SemaphoreType.DMA((parts, 3, SIDE)),
            pltpu.SemaphoreType.DMA((parts, 3, SIDE)),
            pltpu.SemaphoreType.DMA((parts, 3)),
            pltpu.SemaphoreType.DMA((parts, 3)),
        ],
        compiler_params=pltpu.CompilerParams(collective_id=2, has_side_effects=True),
    )(*sums)[:parts]


def tile_kernel(row_of, col_of, slot_of, u_ref, obs_ref, v_hbm, rows_ref, *refs):
    parts = len(ROW_CUTS)
    part_hbm, (v_buf, part_buf, in_sem, out_sem) = refs[:parts], refs[parts:]
    step = pl.program_id(0)
    steps = pl.num_programs(0)
    now = lax.rem(step, 2)
    tiles = steps * STEP_TILES

    def fetch(at, slot, lane):
        return pltpu.make_async_copy(
            v_hbm.at[col_of[at * STEP_TILES + lane]], v_buf.at[slot, lane], in_sem.at[slot, lane]
        )

    def put(at, slot, lane):
        return [
            pltpu.make_async_copy(
                part_buf.at[slot, lane, pl.ds(*cut)],
                part_hbm[part].at[slot_of[part * tiles + at * STEP_TILES + lane]],
                out_sem.at[part, slot, lane],
            )
            for part, cut in enumerate(ROW_CUTS)
        ]

    @pl.when(step == 0)
    def _():
        rows_ref[...] = jnp.zeros_like(rows_ref)
        for lane in range(STEP_TILES):
            fetch(0, 0, lane).start()

    @pl.when(step + 1 < steps)
    def _():
        for lane in range(STEP_TILES):
            fetch(step + 1, 1 - now, lane).start()

    @pl.when(step >= 2)
    def _():
        for lane in range(STEP_TILES):
            for copy in put(step - 2, now, lane):
                copy.wait()

    for lane in range(STEP_TILES):
        fetch(step, now, lane).wait()
    for lane in range(STEP_TILES):
        block = row_of[step * STEP_TILES + lane]
        u = u_ref[block]
        v = v_buf[now, lane]
        residual = lax.dot_general(
            u, v, (((1,), (1,)), ((), ())), preferred_element_type=jnp.float32
        ) - obs_ref[lane].astype(jnp.float32)
        slopes = (residual * lax.rsqrt(residual * residual + smooth_width * smooth_width)).astype(jnp.bfloat16)
        rows_ref[block] += jnp.dot(slopes, v, preferred_element_type=jnp.float32)
        part_buf[now, lane] = lax.dot_general(
            slopes, u, (((0,), (0,)), ((), ())), preferred_element_type=jnp.float32
        ).astype(jnp.bfloat16)
    for lane in range(STEP_TILES):
        for copy in put(step, now, lane):
            copy.start()

    @pl.when(step + 1 == steps)
    def _():
        for lane in range(STEP_TILES):
            for copy in put(step - 1, 1 - now, lane) + put(step, now, lane):
                copy.wait()


def tile_terms(row_of, col_of, slot_of, row_blocks, observed, col_blocks, slots):
    tiles, side, _ = observed.shape
    blocks, _, rank = row_blocks.shape
    parts = len(ROW_CUTS)
    hbm = pl.BlockSpec(memory_space=pltpu.HBM)
    return pl.pallas_call(
        tile_kernel,
        out_shape=(
            jax.ShapeDtypeStruct((blocks, side, rank), jnp.float32),
            *(jax.ShapeDtypeStruct((slots, size, rank), jnp.bfloat16) for _, size in ROW_CUTS),
        ),
        grid_spec=pltpu.PrefetchScalarGridSpec(
            num_scalar_prefetch=3,
            grid=(tiles // STEP_TILES,),
            in_specs=[
                pl.BlockSpec((blocks, side, rank), lambda i, *_: (0, 0, 0)),
                pl.BlockSpec((STEP_TILES, side, side), lambda i, *_: (i, 0, 0)),
                hbm,
            ],
            out_specs=(pl.BlockSpec((blocks, side, rank), lambda i, *_: (0, 0, 0)),) + (hbm,) * parts,
            scratch_shapes=[
                pltpu.VMEM((2, STEP_TILES, side, rank), jnp.bfloat16),
                pltpu.VMEM((2, STEP_TILES, side, rank), jnp.bfloat16),
                pltpu.SemaphoreType.DMA((2, STEP_TILES)),
                pltpu.SemaphoreType.DMA((parts, 2, STEP_TILES)),
            ],
        ),
        compiler_params=pltpu.CompilerParams(vmem_limit_bytes=60 << 20),
        cost_estimate=pl.CostEstimate(
            flops=6 * tiles * side * side * rank, bytes_accessed=4 * tiles * side * side, transcendentals=0
        ),
    )(row_of, col_of, slot_of, row_blocks, observed, col_blocks)


def block_kernel(ids, *refs):
    parts = len(ROW_CUTS)
    sources, targets, totals = refs[:parts], refs[parts : 2 * parts], refs[2 * parts :]
    step = pl.program_id(0)
    bins = pl.num_programs(0)

    @pl.when(step == 0)
    def _():
        for total in totals:
            total[...] = jnp.zeros_like(total)

    def add(lane, carry):
        for part in range(parts):
            block = ids[(part * bins + step) * 128 + lane]

            @pl.when(block >= 0)
            def _(part=part, block=block):
                totals[part][block] += sources[part][lane].astype(jnp.float32)

        return carry

    lax.fori_loop(0, BIN, add, 0)

    @pl.when(step + 1 == bins)
    def _():
        for part in range(parts):
            targets[part][...] = totals[part][...].astype(jnp.bfloat16)


def block_sums(ids, sources, blocks):
    rank = sources[0].shape[-1]
    whole = tuple((blocks, size, rank) for _, size in ROW_CUTS)
    return pl.pallas_call(
        block_kernel,
        out_shape=tuple(jax.ShapeDtypeStruct(shape, jnp.bfloat16) for shape in whole),
        grid_spec=pltpu.PrefetchScalarGridSpec(
            num_scalar_prefetch=1,
            grid=(sources[0].shape[0] // BIN,),
            in_specs=[pl.BlockSpec((BIN, size, rank), lambda i, *_: (i, 0, 0)) for _, size in ROW_CUTS],
            out_specs=tuple(
                pl.BlockSpec(shape, lambda i, *_: (0, 0, 0), pipeline_mode=pl.Buffered(1)) for shape in whole
            ),
            scratch_shapes=[pltpu.VMEM(shape, jnp.float32) for shape in whole],
        ),
        compiler_params=pltpu.CompilerParams(vmem_limit_bytes=60 << 20),
    )(ids, *sources)


def column_kernel(factor_ref, *refs):
    *sources, out_ref = refs
    for (low, size), source in zip(ROW_CUTS, sources):
        rows = pl.ds(low, size)
        total = source[0, 0].astype(jnp.float32)
        for sender in range(1, source.shape[0]):
            total += source[sender, 0].astype(jnp.float32)
        out_ref[0, rows] = factor_ref[0, rows].astype(jnp.float32) - step_rate * total


def column_step(factor, sums):
    held, side, rank = factor.shape
    block = pl.BlockSpec((1, side, rank), lambda i: (i, 0, 0))
    return pl.pallas_call(
        column_kernel,
        out_shape=jax.ShapeDtypeStruct(factor.shape, jnp.float32),
        grid=(held,),
        in_specs=[block]
        + [pl.BlockSpec((SIDE * SIDE, 1, size, rank), lambda i: (0, i, 0, 0)) for _, size in ROW_CUTS],
        out_specs=block,
        compiler_params=pltpu.CompilerParams(vmem_limit_bytes=60 << 20),
    )(factor, *sums)


def body(factor_rows, factor_cols, observed, tile_row, tile_owner, tile_sub):
    tiles, side, _ = observed.shape
    rank = factor_rows.shape[1]
    peers = lax.axis_size(("rows", "cols"))
    held = factor_cols.shape[0] // side
    owners = tile_owner[:, 0]
    codes = owners * held + tile_sub
    spots = {
        0: owners // (SIDE * SIDE * CORES),
        1: owners // (SIDE * CORES) % SIDE,
        2: owners // SIDE % CORES,
        3: owners % SIDE,
    }
    bins = jnp.stack([spots[first] * CORES + spots[2] for first, _, _ in ORDERS])
    blocks = jnp.stack([(spots[second] * SIDE + spots[third]) * held + tile_sub for _, second, third in ORDERS])
    order = jnp.arange(tiles, dtype=jnp.int32)
    earlier = (bins[:, :, None] == bins[:, None, :]) & (order[None, None, :] < order[None, :, None])
    slot_of = bins * BIN + jnp.sum(earlier.astype(jnp.int32), axis=2)
    slots = CORES * SIDE * BIN
    place = jnp.arange(slots, dtype=jnp.int32)
    ids = jnp.max(
        jnp.where(slot_of[:, None, :] == place[None, :, None], blocks[:, None, :], -1), axis=2
    ).reshape(len(ORDERS) * CORES * SIDE, 1, BIN)
    ids = jnp.pad(ids, ((0, 0), (0, 0), (0, 128 - BIN)), constant_values=-1)

    columns = gather_all(factor_cols).reshape(peers * held, side, rank)
    row_part, *parts = tile_terms(
        tile_row,
        codes,
        slot_of.reshape(-1),
        factor_rows.reshape(-1, side, rank),
        observed,
        columns,
        slots,
    )
    row_total = lax.psum(row_part.reshape(-1, rank), "cols")
    ids_here, *parts_here = line_exchange(ids, parts)
    sums = block_sums(ids_here.reshape(-1), parts_here, SIDE * SIDE * held)
    sums = plane_exchange([a.reshape(SIDE, SIDE, held, *a.shape[1:]) for a in sums])
    cols_new = column_step(
        factor_cols.reshape(held, side, rank), [a.reshape(SIDE * SIDE, *a.shape[2:]) for a in sums]
    ).reshape(-1, rank)
    rows_new = factor_rows.astype(jnp.float32) - step_rate * row_total
    return (rows_new, cols_new)


def solution(mesh):
    return jax.shard_map(
        body,
        mesh=mesh,
        in_specs=(
            P("rows", None),
            P(("rows", "cols"), None),
            P(("rows", "cols"), None, None),
            P(("rows", "cols")),
            P(("rows", "cols"), None),
            P(("rows", "cols")),
        ),
        out_specs=(P("rows", None), P(("rows", "cols"), None)),
        check_vma=False,
    )
```

```python
import functools

import jax
import jax.numpy as jnp
from jax import lax
from jax.experimental import pallas as pl
from jax.experimental.pallas import tpu as pltpu
from jax.sharding import PartitionSpec as P

MESH = pl.DeviceIdType.MESH
step_rate = 0.02
smooth_width = 0.5
SIDE = 4
CORES = 2
STEP_TILES = 16
ROW_CUTS = ((0, 88), (88, 88), (176, 80))
BIN = 2 * SIDE * SIDE


def position():
    rows = lax.axis_index("rows")
    return (
        lax.div(rows, SIDE * CORES),
        lax.rem(lax.div(rows, CORES), SIDE),
        lax.rem(rows, CORES),
        lax.axis_index("cols"),
    )


def device_at(y, x, core, z):
    return ((y * SIDE + x) * CORES + core, z)


AXES = (0, 1, 3)
ORDERS = ((0, 1, 3), (1, 3, 0), (3, 0, 1))


def gather_kernel(
    cuts, v_ref, o_ref, held, own_sem, send_sem, recv_sem, slab_send, slab_recv, chip_send, chip_recv
):
    me = position()

    def moved(axis, by):
        there = list(me)
        there[axis] = lax.rem(there[axis] + (by + SIDE), SIDE)
        return tuple(there)

    partner = (me[0], me[1], 1 - me[2], me[3])
    neighbours = [moved(axis, by) for axis in AXES for by in (1, -1)] + [partner]

    load = pltpu.make_async_copy(v_ref, held, own_sem.at[0])
    load.start()
    barrier = pltpu.get_barrier_semaphore()
    for there in neighbours:
        pl.semaphore_signal(barrier, inc=1, device_id=device_at(*there), device_id_type=MESH)
    pl.semaphore_wait(barrier, len(neighbours))
    load.wait()
    own = pltpu.make_async_copy(held, o_ref.at[me], own_sem.at[1])
    own.start()

    def region(part, stage, by, half):
        order = ORDERS[part]
        low, size = cuts[part]
        where = list(me)
        for axis in order[:stage]:
            where[axis] = pl.ds(0, SIDE)
        where[order[stage]] = lax.rem(me[order[stage]] + (by + SIDE), SIDE)
        if half is not None:
            if stage == 0:
                first = size // 32 * 16
                low, size = (low, first) if half == 0 else (low + first, size - first)
            else:
                where[order[stage - 1]] = pl.ds(half * (SIDE // 2), SIDE // 2)
        return o_ref.at[tuple(where) + (pl.ds(low, size),)]

    def send(part, stage, step, way, by, half):
        block = region(part, stage, by, half)
        return pltpu.make_async_remote_copy(
            src_ref=held.at[pl.ds(*cuts[part])] if stage == step == 0 else block,
            dst_ref=block,
            send_sem=send_sem.at[part, stage, step, way],
            recv_sem=recv_sem.at[part, stage, step, way],
            device_id=device_at(*moved(ORDERS[part][stage], 1 if way == 0 else -1)),
            device_id_type=MESH,
        )

    def arrival(part, stage, step, way):
        by = (-1 if way == 0 else 1) * (step + 1)
        block = region(part, stage, by, None if step == 0 else way)
        return pltpu.make_async_remote_copy(
            src_ref=block,
            dst_ref=block,
            send_sem=send_sem.at[part, stage, step, way],
            recv_sem=recv_sem.at[part, stage, step, way],
            device_id=device_at(*moved(ORDERS[part][stage], 1 if way == 0 else -1)),
            device_id_type=MESH,
        )

    def slab(part, core, by, place):
        order = ORDERS[part]
        where = list(me)
        where[2] = core
        where[order[0]] = pl.ds(0, SIDE)
        where[order[1]] = lax.rem(me[order[1]] + ((0, SIDE - 1, 1, 2)[place]), SIDE)
        where[order[2]] = lax.rem(me[order[2]] + (by + SIDE), SIDE)
        return o_ref.at[tuple(where) + (pl.ds(*cuts[part]),)]

    def pass_on(part, place, way, by):
        block = slab(part, me[2], by, place)
        return pltpu.make_async_remote_copy(
            src_ref=block,
            dst_ref=block,
            send_sem=slab_send.at[part, place, way, abs(by)],
            recv_sem=slab_recv.at[part, place, way, abs(by)],
            device_id=device_at(*moved(ORDERS[part][2], 1 if way == 0 else -1)),
            device_id_type=MESH,
        )

    def passed(part, place, way, step):
        block = slab(part, me[2], (-1 if way == 0 else 1) * (step + 1), place)
        return pltpu.make_async_remote_copy(
            src_ref=block,
            dst_ref=block,
            send_sem=slab_send.at[part, place, way, step],
            recv_sem=slab_recv.at[part, place, way, step],
            device_id=device_at(*moved(ORDERS[part][2], 1 if way == 0 else -1)),
            device_id_type=MESH,
        )

    def across(part, place, piece, core):
        block = slab(part, core, (0, -1, 1, 2)[piece], place)
        return pltpu.make_async_remote_copy(
            src_ref=block,
            dst_ref=block,
            send_sem=chip_send.at[part, place, piece],
            recv_sem=chip_recv.at[part, place, piece],
            device_id=device_at(*partner),
            device_id_type=MESH,
        )

    started = []

    def begin(copy):
        copy.start()
        started.append(copy)

    parts = range(len(ORDERS))
    def hand_on(part, place):
        for way in (0, 1):
            begin(pass_on(part, place, way, 0))
        begin(across(part, place, 0, me[2]))

    def receive(part, place):
        for way in (0, 1):
            passed(part, place, way, 0).wait_recv()
            if place % 2 == way:
                begin(pass_on(part, place, way, -1 if way == 0 else 1))
            begin(across(part, place, 1 + way, me[2]))

    for stage in range(2):
        for part in parts:
            for way in (0, 1):
                begin(send(part, stage, 0, way, 0, None))
        if stage == 1:
            for part in parts:
                hand_on(part, 0)
        for part in parts:
            for way in (0, 1):
                arrival(part, stage, 0, way).wait_recv()
                begin(send(part, stage, 1, way, -1 if way == 0 else 1, way))
        if stage == 1:
            for place in (1, 2):
                for part in parts:
                    hand_on(part, place)
        for part in parts:
            for way in (0, 1):
                arrival(part, stage, 1, way).wait_recv()
            if stage == 1:
                hand_on(part, 3)
        if stage == 0:
            own.wait()
    places = (0, 1, 2, 3)
    for place in places:
        for part in parts:
            receive(part, place)
    for place in places:
        for part in parts:
            passed(part, place, place % 2, 1).wait_recv()
            begin(across(part, place, 3, me[2]))
    for place in places:
        for part in parts:
            for piece in range(4):
                across(part, place, piece, 1 - me[2]).wait_recv()
    for copy in started:
        copy.wait_send()


def gather_all(shard):
    rows, rank = shard.shape
    third = rows // 48 * 16
    cuts = ((0, third + 16), (third + 16, third + 16), (2 * third + 32, rows - 2 * third - 32))
    return pl.pallas_call(
        functools.partial(gather_kernel, cuts),
        out_shape=jax.ShapeDtypeStruct((SIDE, SIDE, CORES, SIDE, rows, rank), shard.dtype),
        in_specs=[pl.BlockSpec(memory_space=pltpu.HBM)],
        out_specs=pl.BlockSpec(memory_space=pltpu.HBM),
        scratch_shapes=[
            pltpu.VMEM((rows, rank), shard.dtype),
            pltpu.SemaphoreType.DMA((2,)),
            pltpu.SemaphoreType.DMA((3, 2, 2, 2)),
            pltpu.SemaphoreType.DMA((3, 2, 2, 2)),
            pltpu.SemaphoreType.DMA((3, 4, 2, 2)),
            pltpu.SemaphoreType.DMA((3, 4, 2, 2)),
            pltpu.SemaphoreType.DMA((3, 4, 4)),
            pltpu.SemaphoreType.DMA((3, 4, 4)),
        ],
        compiler_params=pltpu.CompilerParams(collective_id=0, has_side_effects=True),
    )(shard)


def line_kernel(ids_ref, *refs):
    parts = len(ORDERS)
    sources, (ids_out, *targets) = refs[:parts], refs[parts : 2 * parts + 1]
    held = refs[2 * parts + 1 : 3 * parts + 2]
    own_sem, send_sem, recv_sem, ids_send, ids_recv = refs[3 * parts + 2 :]
    me = position()
    offsets = ((1, 0), (3, 0), (2, 0), (1, 1), (3, 1), (2, 1), (0, 1))

    def moved(part, by, flip):
        there = list(me)
        axis = ORDERS[part][0]
        there[axis] = lax.rem(there[axis] + by, SIDE)
        there[2] = 1 - me[2] if flip else me[2]
        return tuple(there)

    def bin_of(part, there):
        return there[ORDERS[part][0]] * CORES + there[2]

    def slots(at):
        return pl.ds(pl.multiple_of(at * BIN, BIN), BIN)

    loads, copies = [], []
    for part in range(parts):
        here = bin_of(part, me)
        line = part * CORES * SIDE + here
        loads.append(pltpu.make_async_copy(sources[part].at[slots(here)], held[part], own_sem.at[part, 0]))
        loads.append(pltpu.make_async_copy(ids_ref.at[line], held[parts].at[part], own_sem.at[part, 1]))
        copies.append(pltpu.make_async_copy(held[part], targets[part].at[slots(here)], own_sem.at[part, 2]))
        copies.append(pltpu.make_async_copy(held[parts].at[part], ids_out.at[line], own_sem.at[part, 3]))
    for copy in loads:
        copy.start()

    greeted = [moved(part, *offset) for part in range(parts) for offset in offsets[:-1]]
    greeted.append(moved(0, 0, 1))
    barrier = pltpu.get_barrier_semaphore()
    for there in greeted:
        pl.semaphore_signal(barrier, inc=1, device_id=device_at(*there), device_id_type=MESH)
    pl.semaphore_wait(barrier, len(greeted))

    def trade(part, place, start):
        by, flip = offsets[place]
        to, source = moved(part, by, flip), moved(part, SIDE - by if by else 0, flip)
        line = part * CORES * SIDE
        filled = bin_of(part, me) if start else bin_of(part, source)
        taken = bin_of(part, to)
        return (
            pltpu.make_async_remote_copy(
                src_ref=sources[part].at[slots(taken)],
                dst_ref=targets[part].at[slots(filled)],
                send_sem=send_sem.at[part, place],
                recv_sem=recv_sem.at[part, place],
                device_id=device_at(*to),
                device_id_type=MESH,
            ),
            pltpu.make_async_remote_copy(
                src_ref=ids_ref.at[line + taken],
                dst_ref=ids_out.at[line + filled],
                send_sem=ids_send.at[part, place],
                recv_sem=ids_recv.at[part, place],
                device_id=device_at(*to),
                device_id_type=MESH,
            ),
        )

    for places in ((0, 1), (2,), (6,), (3, 4), (5,)):
        for part in range(parts):
            for place in places:
                for copy in trade(part, place, True):
                    copy.start()
    for load, copy in zip(loads, copies):
        load.wait()
        copy.start()
    for place in range(len(offsets)):
        for part in range(parts):
            for copy in trade(part, place, False):
                copy.wait_recv()
            for copy in trade(part, place, True):
                copy.wait_send()
    for copy in copies:
        copy.wait()


def line_exchange(ids, sources):
    spec = pl.BlockSpec(memory_space=pltpu.HBM)
    parts = len(sources)
    return pl.pallas_call(
        line_kernel,
        out_shape=tuple(jax.ShapeDtypeStruct(a.shape, a.dtype) for a in (ids, *sources)),
        in_specs=[spec] * (parts + 1),
        out_specs=(spec,) * (parts + 1),
        scratch_shapes=[pltpu.VMEM((BIN, *a.shape[1:]), a.dtype) for a in sources]
        + [pltpu.VMEM((parts, *ids.shape[1:]), ids.dtype), pltpu.SemaphoreType.DMA((parts, 4))]
        + [pltpu.SemaphoreType.DMA((parts, 7))] * 4,
        compiler_params=pltpu.CompilerParams(collective_id=1, has_side_effects=True),
    )(ids, *sources)


def plane_kernel(*refs):
    parts = len(ORDERS)
    sources, targets, between = refs[:parts], refs[parts : 2 * parts], refs[2 * parts : 3 * parts]
    held, late_held = refs[3 * parts : 4 * parts], refs[4 * parts : 5 * parts]
    own_sem, late_sem, first_send, first_recv, then_send, then_recv = refs[5 * parts :]
    me = position()
    hops = (1, 3, 2)

    def moved(axis, by):
        there = list(me)
        there[axis] = lax.rem(there[axis] + by, SIDE)
        return tuple(there)

    loads, own = [], []
    for part in range(parts):
        at = me[ORDERS[part][1]]
        loads.append(pltpu.make_async_copy(sources[part].at[at], held[part], own_sem.at[part, 0]))
        own.append(pltpu.make_async_copy(held[part], between[part].at[at], own_sem.at[part, 1]))
    for copy in loads:
        copy.start()

    greeted = [moved(axis, by) for axis in AXES for by in hops]
    barrier = pltpu.get_barrier_semaphore()
    for there in greeted:
        pl.semaphore_signal(barrier, inc=1, device_id=device_at(*there), device_id_type=MESH)
    pl.semaphore_wait(barrier, len(greeted))

    def first(part, hop, turn, start):
        _, axis, last = ORDERS[part]
        by = hops[hop]
        to = moved(axis, by)
        filled = me[axis] if start else moved(axis, SIDE - by)[axis]
        row = lax.rem(me[last] + turn, SIDE)
        return pltpu.make_async_remote_copy(
            src_ref=sources[part].at[to[axis], row],
            dst_ref=between[part].at[filled, row],
            send_sem=first_send.at[part, hop, turn],
            recv_sem=first_recv.at[part, hop, turn],
            device_id=device_at(*to),
            device_id_type=MESH,
        )

    def then(part, hop, start):
        last = ORDERS[part][2]
        by = hops[hop]
        to = moved(last, by)
        filled = me[last] if start else moved(last, SIDE - by)[last]
        return pltpu.make_async_remote_copy(
            src_ref=between[part].at[:, to[last]],
            dst_ref=targets[part].at[:, filled],
            send_sem=then_send.at[part, hop],
            recv_sem=then_recv.at[part, hop],
            device_id=device_at(*to),
            device_id_type=MESH,
        )

    turns = hops + (0,)
    for turn in turns:
        for places in ((0, 1), (2,)):
            for part in range(parts):
                for hop in places:
                    first(part, hop, turn, True).start()
    for load, copy in zip(loads, own):
        load.wait()
        copy.start()
    for copy in own:
        copy.wait()
    for place, turn in enumerate(turns):
        for part in range(parts):
            for hop in range(len(hops)):
                first(part, hop, turn, False).wait_recv()
            if turn:
                then(part, place, True).start()
    late = []
    for part in range(parts):
        at = me[ORDERS[part][2]]
        load = pltpu.make_async_copy(between[part].at[:, at], late_held[part], late_sem.at[part, 0])
        load.start()
        copy = pltpu.make_async_copy(late_held[part], targets[part].at[:, at], late_sem.at[part, 1])
        late.append((load, copy))
    for load, copy in late:
        load.wait()
        copy.start()
    for part in range(parts):
        for hop in range(len(hops)):
            then(part, hop, False).wait_recv()
            then(part, hop, True).wait_send()
            for turn in turns:
                first(part, hop, turn, True).wait_send()
    for _, copy in late:
        copy.wait()


def plane_exchange(sums):
    spec = pl.BlockSpec(memory_space=pltpu.HBM)
    parts = len(sums)
    shapes = tuple(jax.ShapeDtypeStruct(a.shape, a.dtype) for a in sums)
    return pl.pallas_call(
        plane_kernel,
        out_shape=shapes * 2,
        in_specs=[spec] * parts,
        out_specs=(spec,) * (2 * parts),
        scratch_shapes=[pltpu.VMEM(a.shape[1:], a.dtype) for a in sums] * 2
        + [
            pltpu.SemaphoreType.DMA((parts, 2)),
            pltpu.SemaphoreType.DMA((parts, 2)),
            pltpu.SemaphoreType.DMA((parts, 3, SIDE)),
            pltpu.SemaphoreType.DMA((parts, 3, SIDE)),
            pltpu.SemaphoreType.DMA((parts, 3)),
            pltpu.SemaphoreType.DMA((parts, 3)),
        ],
        compiler_params=pltpu.CompilerParams(collective_id=2, has_side_effects=True),
    )(*sums)[:parts]


def tile_kernel(row_of, col_of, slot_of, u_ref, obs_ref, v_hbm, rows_ref, *refs):
    parts = len(ROW_CUTS)
    part_hbm, part_buf, (v_buf, in_sem, out_sem) = refs[:parts], refs[parts : 2 * parts], refs[2 * parts :]
    step = pl.program_id(0)
    steps = pl.num_programs(0)
    now = lax.rem(step, 2)
    tiles = steps * STEP_TILES

    def fetch(at, slot, lane):
        return pltpu.make_async_copy(
            v_hbm.at[col_of[at * STEP_TILES + lane]], v_buf.at[slot, lane], in_sem.at[slot, lane]
        )

    def put(at, slot, lane):
        return [
            pltpu.make_async_copy(
                part_buf[part].at[slot, lane],
                part_hbm[part].at[slot_of[part * tiles + at * STEP_TILES + lane]],
                out_sem.at[part, slot, lane],
            )
            for part in range(parts)
        ]

    @pl.when(step == 0)
    def _():
        rows_ref[...] = jnp.zeros_like(rows_ref)
        for lane in range(STEP_TILES):
            fetch(0, 0, lane).start()

    @pl.when(step + 1 < steps)
    def _():
        for lane in range(STEP_TILES):
            fetch(step + 1, 1 - now, lane).start()

    @pl.when(step >= 2)
    def _():
        for lane in range(STEP_TILES):
            for copy in put(step - 2, now, lane):
                copy.wait()

    for lane in range(STEP_TILES):
        fetch(step, now, lane).wait()
    lanes = range(STEP_TILES)
    blocks = [row_of[step * STEP_TILES + lane] for lane in lanes]
    us = [u_ref[block] for block in blocks]
    vs = [v_buf[now, lane] for lane in lanes]
    products = [
        lax.dot_general(u, v, (((1,), (1,)), ((), ())), preferred_element_type=jnp.float32)
        for u, v in zip(us, vs)
    ]
    slopes = []
    for lane in lanes:
        residual = products[lane] - obs_ref[lane].astype(jnp.float32)
        slopes.append(
            (residual * lax.rsqrt(residual * residual + smooth_width * smooth_width)).astype(jnp.bfloat16)
        )
    terms = [jnp.dot(slope, v, preferred_element_type=jnp.float32) for slope, v in zip(slopes, vs)]
    for lane in lanes:
        term = lax.dot_general(
            slopes[lane], us[lane], (((0,), (0,)), ((), ())), preferred_element_type=jnp.float32
        )
        for part, (low, size) in enumerate(ROW_CUTS):
            part_buf[part][now, lane] = term[low : low + size].astype(jnp.bfloat16)
    for block, term in zip(blocks, terms):
        rows_ref[block] += term
    for lane in range(STEP_TILES):
        for copy in put(step, now, lane):
            copy.start()

    @pl.when(step + 1 == steps)
    def _():
        for lane in range(STEP_TILES):
            for copy in put(step - 1, 1 - now, lane) + put(step, now, lane):
                copy.wait()


def tile_terms(row_of, col_of, slot_of, row_blocks, observed, col_blocks, slots):
    tiles, side, _ = observed.shape
    blocks, _, rank = row_blocks.shape
    parts = len(ROW_CUTS)
    hbm = pl.BlockSpec(memory_space=pltpu.HBM)
    return pl.pallas_call(
        tile_kernel,
        out_shape=(
            jax.ShapeDtypeStruct((blocks, side, rank), jnp.float32),
            *(jax.ShapeDtypeStruct((slots, size, rank), jnp.bfloat16) for _, size in ROW_CUTS),
        ),
        grid_spec=pltpu.PrefetchScalarGridSpec(
            num_scalar_prefetch=3,
            grid=(tiles // STEP_TILES,),
            in_specs=[
                pl.BlockSpec((blocks, side, rank), lambda i, *_: (0, 0, 0)),
                pl.BlockSpec((STEP_TILES, side, side), lambda i, *_: (i, 0, 0)),
                hbm,
            ],
            out_specs=(pl.BlockSpec((blocks, side, rank), lambda i, *_: (0, 0, 0)),) + (hbm,) * parts,
            scratch_shapes=[pltpu.VMEM((2, STEP_TILES, size, rank), jnp.bfloat16) for _, size in ROW_CUTS]
            + [
                pltpu.VMEM((2, STEP_TILES, side, rank), jnp.bfloat16),
                pltpu.SemaphoreType.DMA((2, STEP_TILES)),
                pltpu.SemaphoreType.DMA((parts, 2, STEP_TILES)),
            ],
        ),
        compiler_params=pltpu.CompilerParams(vmem_limit_bytes=60 << 20),
        cost_estimate=pl.CostEstimate(
            flops=6 * tiles * side * side * rank, bytes_accessed=4 * tiles * side * side, transcendentals=0
        ),
    )(row_of, col_of, slot_of, row_blocks, observed, col_blocks)


def block_kernel(ids, *refs):
    parts = len(ROW_CUTS)
    sources, targets, totals = refs[:parts], refs[parts : 2 * parts], refs[2 * parts :]
    step = pl.program_id(0)
    bins = pl.num_programs(0)

    @pl.when(step == 0)
    def _():
        for total in totals:
            total[...] = jnp.zeros_like(total)

    for part in range(parts):
        line = (part * bins + step) * 128

        def add(lane, carry, part=part, line=line):
            totals[part][ids[line + lane]] += sources[part][lane].astype(jnp.float32)
            return carry

        lax.fori_loop(0, ids[line + BIN], add, 0)

    @pl.when(step + 1 == bins)
    def _():
        for part in range(parts):
            targets[part][...] = totals[part][...].astype(jnp.bfloat16)


def block_sums(ids, sources, blocks):
    rank = sources[0].shape[-1]
    whole = tuple((blocks, size, rank) for _, size in ROW_CUTS)
    return pl.pallas_call(
        block_kernel,
        out_shape=tuple(jax.ShapeDtypeStruct(shape, jnp.bfloat16) for shape in whole),
        grid_spec=pltpu.PrefetchScalarGridSpec(
            num_scalar_prefetch=1,
            grid=(sources[0].shape[0] // BIN,),
            in_specs=[pl.BlockSpec((BIN, size, rank), lambda i, *_: (i, 0, 0)) for _, size in ROW_CUTS],
            out_specs=tuple(
                pl.BlockSpec(shape, lambda i, *_: (0, 0, 0), pipeline_mode=pl.Buffered(1)) for shape in whole
            ),
            scratch_shapes=[pltpu.VMEM(shape, jnp.float32) for shape in whole],
        ),
        compiler_params=pltpu.CompilerParams(vmem_limit_bytes=60 << 20),
    )(ids, *sources)


def column_kernel(factor_ref, *refs):
    *sources, out_ref = refs
    factor = factor_ref[0].astype(jnp.float32)
    for (low, size), source in zip(ROW_CUTS, sources):
        total = source[0, 0].astype(jnp.float32)
        for sender in range(1, source.shape[0]):
            total += source[sender, 0].astype(jnp.float32)
        out_ref[0, pl.ds(low, size)] = factor[low : low + size] - step_rate * total


def column_step(factor, sums):
    held, side, rank = factor.shape
    block = pl.BlockSpec((1, side, rank), lambda i: (i, 0, 0))
    return pl.pallas_call(
        column_kernel,
        out_shape=jax.ShapeDtypeStruct(factor.shape, jnp.float32),
        grid=(held,),
        in_specs=[block]
        + [pl.BlockSpec((SIDE * SIDE, 1, size, rank), lambda i: (0, i, 0, 0)) for _, size in ROW_CUTS],
        out_specs=block,
        compiler_params=pltpu.CompilerParams(vmem_limit_bytes=60 << 20),
    )(factor, *sums)


def body(factor_rows, factor_cols, observed, tile_row, tile_owner, tile_sub):
    tiles, side, _ = observed.shape
    rank = factor_rows.shape[1]
    peers = lax.axis_size(("rows", "cols"))
    held = factor_cols.shape[0] // side
    owners = tile_owner[:, 0]
    codes = owners * held + tile_sub
    spots = {
        0: owners // (SIDE * SIDE * CORES),
        1: owners // (SIDE * CORES) % SIDE,
        2: owners // SIDE % CORES,
        3: owners % SIDE,
    }
    bins = jnp.stack([spots[first] * CORES + spots[2] for first, _, _ in ORDERS])
    blocks = jnp.stack([(spots[second] * SIDE + spots[third]) * held + tile_sub for _, second, third in ORDERS])
    order = jnp.arange(tiles, dtype=jnp.int32)
    earlier = (bins[:, :, None] == bins[:, None, :]) & (order[None, None, :] < order[None, :, None])
    slot_of = bins * BIN + jnp.sum(earlier.astype(jnp.int32), axis=2)
    slots = CORES * SIDE * BIN
    place = jnp.arange(slots, dtype=jnp.int32)
    ids = jnp.max(
        jnp.where(slot_of[:, None, :] == place[None, :, None], blocks[:, None, :], -1), axis=2
    ).reshape(len(ORDERS) * CORES * SIDE, 1, BIN)
    filled = jnp.sum((ids >= 0).astype(jnp.int32), axis=2, keepdims=True)
    ids = jnp.concatenate([ids, jnp.broadcast_to(filled, (*filled.shape[:2], 128 - BIN))], axis=2)

    columns = gather_all(factor_cols).reshape(peers * held, side, rank)
    row_part, *parts = tile_terms(
        tile_row,
        codes,
        slot_of.reshape(-1),
        factor_rows.reshape(-1, side, rank),
        observed,
        columns,
        slots,
    )
    row_total = lax.psum(row_part.reshape(-1, rank), "cols")
    ids_here, *parts_here = line_exchange(ids, parts)
    sums = block_sums(ids_here.reshape(-1), parts_here, SIDE * SIDE * held)
    sums = plane_exchange([a.reshape(SIDE, SIDE, held, *a.shape[1:]) for a in sums])
    cols_new = column_step(
        factor_cols.reshape(held, side, rank), [a.reshape(SIDE * SIDE, *a.shape[2:]) for a in sums]
    ).reshape(-1, rank)
    rows_new = factor_rows.astype(jnp.float32) - step_rate * row_total
    return (rows_new, cols_new)


def solution(mesh):
    return jax.shard_map(
        body,
        mesh=mesh,
        in_specs=(
            P("rows", None),
            P(("rows", "cols"), None),
            P(("rows", "cols"), None, None),
            P(("rows", "cols")),
            P(("rows", "cols"), None),
            P(("rows", "cols")),
        ),
        out_specs=(P("rows", None), P(("rows", "cols"), None)),
        check_vma=False,
    )
```

```python
import functools

import jax
import jax.numpy as jnp
from jax import lax
from jax.experimental import pallas as pl
from jax.experimental.pallas import tpu as pltpu
from jax.sharding import PartitionSpec as P

MESH = pl.DeviceIdType.MESH
step_rate = 0.02
smooth_width = 0.5
SIDE = 4
CORES = 2
STEP_TILES = 16
ROW_CUTS = ((0, 88), (88, 88), (176, 80))
BIN = 2 * SIDE * SIDE
CBD = 8


def position():
    rows = lax.axis_index("rows")
    return (
        lax.div(rows, SIDE * CORES),
        lax.rem(lax.div(rows, CORES), SIDE),
        lax.rem(rows, CORES),
        lax.axis_index("cols"),
    )


def device_at(y, x, core, z):
    return ((y * SIDE + x) * CORES + core, z)


AXES = (0, 1, 3)
ORDERS = ((0, 1, 3), (1, 3, 0), (3, 0, 1))


def request_kernel(ids_ref, v_ref, *refs):
    parts = len(ORDERS)
    ids_out, targets, held, ids_held = refs[0], refs[1 : parts + 1], refs[parts + 1 : 2 * parts + 1], refs[2 * parts + 1]
    own_sem, send_sem, recv_sem, ids_send, ids_recv = refs[2 * parts + 2 :]
    me = position()

    def moved(axis, by, flip=0):
        there = list(me)
        there[axis] = lax.rem(there[axis] + (by + SIDE), SIDE)
        there[2] = 1 - me[2] if flip else me[2]
        return tuple(there)

    def bin_of(part, there):
        return there[ORDERS[part][0]] * CORES + there[2]

    loads, own = [], []
    for part, cut in enumerate(ROW_CUTS):
        _, first, second = ORDERS[part]
        line = part * CORES * SIDE + bin_of(part, me)
        loads.append(pltpu.make_async_copy(v_ref.at[:, pl.ds(*cut)], held[part], own_sem.at[part, 0]))
        own.append(pltpu.make_async_copy(held[part], targets[part].at[me[first], me[second]], own_sem.at[part, 1]))
        loads.append(pltpu.make_async_copy(ids_ref.at[line], ids_held.at[part], own_sem.at[part, 2]))
        own.append(pltpu.make_async_copy(ids_held.at[part], ids_out.at[line], own_sem.at[part, 3]))
    for copy in loads:
        copy.start()

    offsets = ((1, 0), (3, 0), (2, 0), (1, 1), (3, 1), (2, 1), (0, 1))
    greeted = [moved(axis, by, flip) for axis in AXES for by, flip in offsets[:-1]]
    greeted.append(moved(0, 0, 1))
    barrier = pltpu.get_barrier_semaphore()
    for there in greeted:
        pl.semaphore_signal(barrier, inc=1, device_id=device_at(*there), device_id_type=MESH)
    pl.semaphore_wait(barrier, len(greeted))
    for copy in loads:
        copy.wait()
    for copy in own:
        copy.start()

    def ask(part, place, start):
        by, flip = offsets[place]
        axis = ORDERS[part][0]
        to, source = moved(axis, by, flip), moved(axis, -by, flip)
        line = part * CORES * SIDE
        return pltpu.make_async_remote_copy(
            src_ref=ids_ref.at[line + bin_of(part, to)],
            dst_ref=ids_out.at[line + (bin_of(part, me) if start else bin_of(part, source))],
            send_sem=ids_send.at[part, place],
            recv_sem=ids_recv.at[part, place],
            device_id=device_at(*to),
            device_id_type=MESH,
        )

    def region(part, stage, by, half):
        _, first, second = ORDERS[part]
        low = 0 if half is None else half
        if stage == 0:
            at = (moved(first, by)[first], me[second])
            cut = pl.ds(0, CBD) if half is None else pl.ds(low * (CBD // 2), CBD // 2)
            return targets[part].at[at + (cut,)]
        cut = pl.ds(0, SIDE) if half is None else pl.ds(low * (SIDE // 2), SIDE // 2)
        return targets[part].at[cut, moved(second, by)[second]]

    def copy_of(part, stage, step, way, block, source=None):
        return pltpu.make_async_remote_copy(
            src_ref=block if source is None else source,
            dst_ref=block,
            send_sem=send_sem.at[part, stage, step, way],
            recv_sem=recv_sem.at[part, stage, step, way],
            device_id=device_at(*moved(ORDERS[part][stage + 1], 1 if way == 0 else -1)),
            device_id_type=MESH,
        )

    def send(part, stage, step, way):
        by = 0 if step == 0 else (-1 if way == 0 else 1)
        block = region(part, stage, by, None if step == 0 else way)
        return copy_of(part, stage, step, way, block, held[part] if stage == step == 0 else None)

    def arrival(part, stage, step, way):
        by = (-1 if way == 0 else 1) * (step + 1)
        return copy_of(part, stage, step, way, region(part, stage, by, None if step == 0 else way))

    started = []

    def begin(copy):
        copy.start()
        started.append(copy)

    for stage in range(2):
        for part in range(parts):
            for way in (0, 1):
                begin(send(part, stage, 0, way))
        if stage == 0:
            for place in range(len(offsets)):
                for part in range(parts):
                    begin(ask(part, place, True))
        for part in range(parts):
            for way in (0, 1):
                arrival(part, stage, 0, way).wait_recv()
                begin(send(part, stage, 1, way))
        for part in range(parts):
            for way in (0, 1):
                arrival(part, stage, 1, way).wait_recv()
        if stage == 0:
            for copy in own:
                copy.wait()
    for place in range(len(offsets)):
        for part in range(parts):
            ask(part, place, False).wait_recv()
    for copy in started:
        copy.wait_send()


def request_blocks(ids, blocks):
    held, _, rank = blocks.shape
    parts = len(ROW_CUTS)
    spec = pl.BlockSpec(memory_space=pltpu.HBM)
    return pl.pallas_call(
        request_kernel,
        out_shape=(
            jax.ShapeDtypeStruct(ids.shape, ids.dtype),
            *(jax.ShapeDtypeStruct((SIDE, SIDE, held, size, rank), blocks.dtype) for _, size in ROW_CUTS),
        ),
        in_specs=[spec, spec],
        out_specs=(spec,) * (parts + 1),
        scratch_shapes=[pltpu.VMEM((held, size, rank), blocks.dtype) for _, size in ROW_CUTS]
        + [
            pltpu.VMEM((parts, *ids.shape[1:]), ids.dtype),
            pltpu.SemaphoreType.DMA((parts, 4)),
            pltpu.SemaphoreType.DMA((parts, 2, 2, 2)),
            pltpu.SemaphoreType.DMA((parts, 2, 2, 2)),
            pltpu.SemaphoreType.DMA((parts, 7)),
            pltpu.SemaphoreType.DMA((parts, 7)),
        ],
        compiler_params=pltpu.CompilerParams(collective_id=0, has_side_effects=True),
    )(ids, blocks)


def serve_kernel(ids, *refs):
    parts = len(ROW_CUTS)
    sources, targets = refs[:parts], refs[parts:]
    step = pl.program_id(0)
    bins = pl.num_programs(0)
    for part in range(parts):
        line = (part * bins + step) * 128

        def fill(lane, carry, part=part, line=line):
            targets[part][lane] = sources[part][ids[line + lane]]
            return carry

        lax.fori_loop(0, ids[line + BIN], fill, 0)


def serve_blocks(ids, sources, slots):
    blocks, _, rank = sources[0].shape
    return pl.pallas_call(
        serve_kernel,
        out_shape=tuple(jax.ShapeDtypeStruct((slots, size, rank), jnp.bfloat16) for _, size in ROW_CUTS),
        grid_spec=pltpu.PrefetchScalarGridSpec(
            num_scalar_prefetch=1,
            grid=(slots // BIN,),
            in_specs=[
                pl.BlockSpec((blocks, size, rank), lambda i, *_: (0, 0, 0), pipeline_mode=pl.Buffered(1))
                for _, size in ROW_CUTS
            ],
            out_specs=tuple(pl.BlockSpec((BIN, size, rank), lambda i, *_: (i, 0, 0)) for _, size in ROW_CUTS),
        ),
        compiler_params=pltpu.CompilerParams(vmem_limit_bytes=60 << 20),
    )(ids, *sources)


def line_kernel(*refs):
    parts = len(ORDERS)
    sources, targets, held = refs[:parts], refs[parts : 2 * parts], refs[2 * parts : 3 * parts]
    own_sem, send_sem, recv_sem = refs[3 * parts :]
    me = position()
    offsets = ((1, 0), (3, 0), (2, 0), (1, 1), (3, 1), (2, 1), (0, 1))

    def moved(part, by, flip):
        there = list(me)
        axis = ORDERS[part][0]
        there[axis] = lax.rem(there[axis] + by, SIDE)
        there[2] = 1 - me[2] if flip else me[2]
        return tuple(there)

    def bin_of(part, there):
        return there[ORDERS[part][0]] * CORES + there[2]

    def slots(at):
        return pl.ds(pl.multiple_of(at * BIN, BIN), BIN)

    loads, copies = [], []
    for part in range(parts):
        here = bin_of(part, me)
        loads.append(pltpu.make_async_copy(sources[part].at[slots(here)], held[part], own_sem.at[part, 0]))
        copies.append(pltpu.make_async_copy(held[part], targets[part].at[slots(here)], own_sem.at[part, 1]))
    for copy in loads:
        copy.start()

    greeted = [moved(part, *offset) for part in range(parts) for offset in offsets[:-1]]
    greeted.append(moved(0, 0, 1))
    barrier = pltpu.get_barrier_semaphore()
    for there in greeted:
        pl.semaphore_signal(barrier, inc=1, device_id=device_at(*there), device_id_type=MESH)
    pl.semaphore_wait(barrier, len(greeted))

    def trade(part, place, start):
        by, flip = offsets[place]
        to, source = moved(part, by, flip), moved(part, SIDE - by if by else 0, flip)
        filled = bin_of(part, me) if start else bin_of(part, source)
        return pltpu.make_async_remote_copy(
            src_ref=sources[part].at[slots(bin_of(part, to))],
            dst_ref=targets[part].at[slots(filled)],
            send_sem=send_sem.at[part, place],
            recv_sem=recv_sem.at[part, place],
            device_id=device_at(*to),
            device_id_type=MESH,
        )

    for places in ((0, 1), (2,), (6,), (3, 4), (5,)):
        for part in range(parts):
            for place in places:
                trade(part, place, True).start()
    for load, copy in zip(loads, copies):
        load.wait()
        copy.start()
    for place in range(len(offsets)):
        for part in range(parts):
            trade(part, place, False).wait_recv()
            trade(part, place, True).wait_send()
    for copy in copies:
        copy.wait()


def line_exchange(sources, collective_id):
    spec = pl.BlockSpec(memory_space=pltpu.HBM)
    parts = len(sources)
    return pl.pallas_call(
        line_kernel,
        out_shape=tuple(jax.ShapeDtypeStruct(a.shape, a.dtype) for a in sources),
        in_specs=[spec] * parts,
        out_specs=(spec,) * parts,
        scratch_shapes=[pltpu.VMEM((BIN, *a.shape[1:]), a.dtype) for a in sources]
        + [pltpu.SemaphoreType.DMA((parts, 2))]
        + [pltpu.SemaphoreType.DMA((parts, 7))] * 2,
        compiler_params=pltpu.CompilerParams(collective_id=collective_id, has_side_effects=True),
    )(*sources)


def plane_kernel(*refs):
    parts = len(ORDERS)
    sources, targets, between = refs[:parts], refs[parts : 2 * parts], refs[2 * parts : 3 * parts]
    held, late_held = refs[3 * parts : 4 * parts], refs[4 * parts : 5 * parts]
    own_sem, late_sem, first_send, first_recv, then_send, then_recv = refs[5 * parts :]
    me = position()
    hops = (1, 3, 2)

    def moved(axis, by):
        there = list(me)
        there[axis] = lax.rem(there[axis] + by, SIDE)
        return tuple(there)

    loads, own = [], []
    for part in range(parts):
        at = me[ORDERS[part][1]]
        loads.append(pltpu.make_async_copy(sources[part].at[at], held[part], own_sem.at[part, 0]))
        own.append(pltpu.make_async_copy(held[part], between[part].at[at], own_sem.at[part, 1]))
    for copy in loads:
        copy.start()

    greeted = [moved(axis, by) for axis in AXES for by in hops]
    barrier = pltpu.get_barrier_semaphore()
    for there in greeted:
        pl.semaphore_signal(barrier, inc=1, device_id=device_at(*there), device_id_type=MESH)
    pl.semaphore_wait(barrier, len(greeted))

    def first(part, hop, turn, start):
        _, axis, last = ORDERS[part]
        by = hops[hop]
        to = moved(axis, by)
        filled = me[axis] if start else moved(axis, SIDE - by)[axis]
        row = lax.rem(me[last] + turn, SIDE)
        return pltpu.make_async_remote_copy(
            src_ref=sources[part].at[to[axis], row],
            dst_ref=between[part].at[filled, row],
            send_sem=first_send.at[part, hop, turn],
            recv_sem=first_recv.at[part, hop, turn],
            device_id=device_at(*to),
            device_id_type=MESH,
        )

    def then(part, hop, start):
        last = ORDERS[part][2]
        by = hops[hop]
        to = moved(last, by)
        filled = me[last] if start else moved(last, SIDE - by)[last]
        return pltpu.make_async_remote_copy(
            src_ref=between[part].at[:, to[last]],
            dst_ref=targets[part].at[:, filled],
            send_sem=then_send.at[part, hop],
            recv_sem=then_recv.at[part, hop],
            device_id=device_at(*to),
            device_id_type=MESH,
        )

    turns = hops + (0,)
    for turn in turns:
        for places in ((0, 1), (2,)):
            for part in range(parts):
                for hop in places:
                    first(part, hop, turn, True).start()
    for load, copy in zip(loads, own):
        load.wait()
        copy.start()
    for copy in own:
        copy.wait()
    for place, turn in enumerate(turns):
        for part in range(parts):
            for hop in range(len(hops)):
                first(part, hop, turn, False).wait_recv()
            if turn:
                then(part, place, True).start()
    late = []
    for part in range(parts):
        at = me[ORDERS[part][2]]
        load = pltpu.make_async_copy(between[part].at[:, at], late_held[part], late_sem.at[part, 0])
        load.start()
        copy = pltpu.make_async_copy(late_held[part], targets[part].at[:, at], late_sem.at[part, 1])
        late.append((load, copy))
    for load, copy in late:
        load.wait()
        copy.start()
    for part in range(parts):
        for hop in range(len(hops)):
            then(part, hop, False).wait_recv()
            then(part, hop, True).wait_send()
            for turn in turns:
                first(part, hop, turn, True).wait_send()
    for _, copy in late:
        copy.wait()


def plane_exchange(sums):
    spec = pl.BlockSpec(memory_space=pltpu.HBM)
    parts = len(sums)
    shapes = tuple(jax.ShapeDtypeStruct(a.shape, a.dtype) for a in sums)
    return pl.pallas_call(
        plane_kernel,
        out_shape=shapes * 2,
        in_specs=[spec] * parts,
        out_specs=(spec,) * (2 * parts),
        scratch_shapes=[pltpu.VMEM(a.shape[1:], a.dtype) for a in sums] * 2
        + [
            pltpu.SemaphoreType.DMA((parts, 2)),
            pltpu.SemaphoreType.DMA((parts, 2)),
            pltpu.SemaphoreType.DMA((parts, 3, SIDE)),
            pltpu.SemaphoreType.DMA((parts, 3, SIDE)),
            pltpu.SemaphoreType.DMA((parts, 3)),
            pltpu.SemaphoreType.DMA((parts, 3)),
        ],
        compiler_params=pltpu.CompilerParams(collective_id=2, has_side_effects=True),
    )(*sums)[:parts]


def tile_kernel(row_of, slot_of, u_ref, obs_ref, *refs):
    parts = len(ROW_CUTS)
    v_hbm, (rows_ref, *part_hbm) = refs[:parts], refs[parts : 2 * parts + 1]
    part_buf, v_buf = refs[2 * parts + 1 : 3 * parts + 1], refs[3 * parts + 1 : 4 * parts + 1]
    in_sem, out_sem = refs[4 * parts + 1 :]
    step = pl.program_id(0)
    steps = pl.num_programs(0)
    now = lax.rem(step, 2)
    tiles = steps * STEP_TILES

    def fetch(at, slot, lane):
        return [
            pltpu.make_async_copy(
                v_hbm[part].at[slot_of[part * tiles + at * STEP_TILES + lane]],
                v_buf[part].at[slot, lane],
                in_sem.at[part, slot, lane],
            )
            for part in range(parts)
        ]

    def put(at, slot, lane):
        return [
            pltpu.make_async_copy(
                part_buf[part].at[slot, lane],
                part_hbm[part].at[slot_of[part * tiles + at * STEP_TILES + lane]],
                out_sem.at[part, slot, lane],
            )
            for part in range(parts)
        ]

    @pl.when(step == 0)
    def _():
        rows_ref[...] = jnp.zeros_like(rows_ref)
        for lane in range(STEP_TILES):
            for copy in fetch(0, 0, lane):
                copy.start()

    @pl.when(step + 1 < steps)
    def _():
        for lane in range(STEP_TILES):
            for copy in fetch(step + 1, 1 - now, lane):
                copy.start()

    @pl.when(step >= 2)
    def _():
        for lane in range(STEP_TILES):
            for copy in put(step - 2, now, lane):
                copy.wait()

    for lane in range(STEP_TILES):
        for copy in fetch(step, now, lane):
            copy.wait()
    lanes = range(STEP_TILES)
    blocks = [row_of[step * STEP_TILES + lane] for lane in lanes]
    us = [u_ref[block] for block in blocks]
    vs = [jnp.concatenate([v_buf[part][now, lane] for part in range(parts)], axis=0) for lane in lanes]
    products = [
        lax.dot_general(u, v, (((1,), (1,)), ((), ())), preferred_element_type=jnp.float32)
        for u, v in zip(us, vs)
    ]
    slopes = []
    for lane in lanes:
        residual = products[lane] - obs_ref[lane].astype(jnp.float32)
        slopes.append(
            (residual * lax.rsqrt(residual * residual + smooth_width * smooth_width)).astype(jnp.bfloat16)
        )
    terms = [jnp.dot(slope, v, preferred_element_type=jnp.float32) for slope, v in zip(slopes, vs)]
    for lane in lanes:
        term = lax.dot_general(
            slopes[lane], us[lane], (((0,), (0,)), ((), ())), preferred_element_type=jnp.float32
        )
        for part, (low, size) in enumerate(ROW_CUTS):
            part_buf[part][now, lane] = term[low : low + size].astype(jnp.bfloat16)
    for block, term in zip(blocks, terms):
        rows_ref[block] += term
    for lane in range(STEP_TILES):
        for copy in put(step, now, lane):
            copy.start()

    @pl.when(step + 1 == steps)
    def _():
        for lane in range(STEP_TILES):
            for copy in put(step - 1, 1 - now, lane) + put(step, now, lane):
                copy.wait()


def tile_terms(row_of, slot_of, row_blocks, observed, col_parts):
    tiles, side, _ = observed.shape
    blocks, _, rank = row_blocks.shape
    parts, slots = len(ROW_CUTS), col_parts[0].shape[0]
    hbm = pl.BlockSpec(memory_space=pltpu.HBM)
    return pl.pallas_call(
        tile_kernel,
        out_shape=(
            jax.ShapeDtypeStruct((blocks, side, rank), jnp.float32),
            *(jax.ShapeDtypeStruct((slots, size, rank), jnp.bfloat16) for _, size in ROW_CUTS),
        ),
        grid_spec=pltpu.PrefetchScalarGridSpec(
            num_scalar_prefetch=2,
            grid=(tiles // STEP_TILES,),
            in_specs=[
                pl.BlockSpec((blocks, side, rank), lambda i, *_: (0, 0, 0)),
                pl.BlockSpec((STEP_TILES, side, side), lambda i, *_: (i, 0, 0)),
            ]
            + [hbm] * parts,
            out_specs=(pl.BlockSpec((blocks, side, rank), lambda i, *_: (0, 0, 0)),) + (hbm,) * parts,
            scratch_shapes=[pltpu.VMEM((2, STEP_TILES, size, rank), jnp.bfloat16) for _, size in ROW_CUTS * 2]
            + [
                pltpu.SemaphoreType.DMA((parts, 2, STEP_TILES)),
                pltpu.SemaphoreType.DMA((parts, 2, STEP_TILES)),
            ],
        ),
        compiler_params=pltpu.CompilerParams(vmem_limit_bytes=60 << 20),
        cost_estimate=pl.CostEstimate(
            flops=6 * tiles * side * side * rank, bytes_accessed=4 * tiles * side * side, transcendentals=0
        ),
    )(row_of, slot_of, row_blocks, observed, *col_parts)


def block_kernel(ids, *refs):
    parts = len(ROW_CUTS)
    sources, targets, totals = refs[:parts], refs[parts : 2 * parts], refs[2 * parts :]
    step = pl.program_id(0)
    bins = pl.num_programs(0)

    @pl.when(step == 0)
    def _():
        for total in totals:
            total[...] = jnp.zeros_like(total)

    for part in range(parts):
        line = (part * bins + step) * 128

        def add(lane, carry, part=part, line=line):
            totals[part][ids[line + lane]] += sources[part][lane].astype(jnp.float32)
            return carry

        lax.fori_loop(0, ids[line + BIN], add, 0)

    @pl.when(step + 1 == bins)
    def _():
        for part in range(parts):
            targets[part][...] = totals[part][...].astype(jnp.bfloat16)


def block_sums(ids, sources, blocks):
    rank = sources[0].shape[-1]
    whole = tuple((blocks, size, rank) for _, size in ROW_CUTS)
    return pl.pallas_call(
        block_kernel,
        out_shape=tuple(jax.ShapeDtypeStruct(shape, jnp.bfloat16) for shape in whole),
        grid_spec=pltpu.PrefetchScalarGridSpec(
            num_scalar_prefetch=1,
            grid=(sources[0].shape[0] // BIN,),
            in_specs=[pl.BlockSpec((BIN, size, rank), lambda i, *_: (i, 0, 0)) for _, size in ROW_CUTS],
            out_specs=tuple(
                pl.BlockSpec(shape, lambda i, *_: (0, 0, 0), pipeline_mode=pl.Buffered(1)) for shape in whole
            ),
            scratch_shapes=[pltpu.VMEM(shape, jnp.float32) for shape in whole],
        ),
        compiler_params=pltpu.CompilerParams(vmem_limit_bytes=60 << 20),
    )(ids, *sources)


def column_kernel(factor_ref, *refs):
    *sources, out_ref = refs
    factor = factor_ref[0].astype(jnp.float32)
    for (low, size), source in zip(ROW_CUTS, sources):
        total = source[0, 0].astype(jnp.float32)
        for sender in range(1, source.shape[0]):
            total += source[sender, 0].astype(jnp.float32)
        out_ref[0, pl.ds(low, size)] = factor[low : low + size] - step_rate * total


def column_step(factor, sums):
    held, side, rank = factor.shape
    block = pl.BlockSpec((1, side, rank), lambda i: (i, 0, 0))
    return pl.pallas_call(
        column_kernel,
        out_shape=jax.ShapeDtypeStruct(factor.shape, jnp.float32),
        grid=(held,),
        in_specs=[block]
        + [pl.BlockSpec((SIDE * SIDE, 1, size, rank), lambda i: (0, i, 0, 0)) for _, size in ROW_CUTS],
        out_specs=block,
        compiler_params=pltpu.CompilerParams(vmem_limit_bytes=60 << 20),
    )(factor, *sums)


def body(factor_rows, factor_cols, observed, tile_row, tile_owner, tile_sub):
    tiles, side, _ = observed.shape
    rank = factor_rows.shape[1]
    held = factor_cols.shape[0] // side
    owners = tile_owner[:, 0]
    spots = {
        0: owners // (SIDE * SIDE * CORES),
        1: owners // (SIDE * CORES) % SIDE,
        2: owners // SIDE % CORES,
        3: owners % SIDE,
    }
    bins = jnp.stack([spots[first] * CORES + spots[2] for first, _, _ in ORDERS])
    blocks = jnp.stack([(spots[second] * SIDE + spots[third]) * held + tile_sub for _, second, third in ORDERS])
    order = jnp.arange(tiles, dtype=jnp.int32)
    earlier = (bins[:, :, None] == bins[:, None, :]) & (order[None, None, :] < order[None, :, None])
    slot_of = bins * BIN + jnp.sum(earlier.astype(jnp.int32), axis=2)
    slots = CORES * SIDE * BIN
    place = jnp.arange(slots, dtype=jnp.int32)
    ids = jnp.max(
        jnp.where(slot_of[:, None, :] == place[None, :, None], blocks[:, None, :], -1), axis=2
    ).reshape(len(ORDERS) * CORES * SIDE, 1, BIN)
    filled = jnp.sum((ids >= 0).astype(jnp.int32), axis=2, keepdims=True)
    ids = jnp.concatenate([ids, jnp.broadcast_to(filled, (*filled.shape[:2], 128 - BIN))], axis=2)

    ids_here, *plane = request_blocks(ids, factor_cols.reshape(held, side, rank))
    ids_here = ids_here.reshape(-1)
    plane = [a.reshape(-1, *a.shape[3:]) for a in plane]
    columns = line_exchange(serve_blocks(ids_here, plane, slots), 1)
    row_part, *parts = tile_terms(
        tile_row, slot_of.reshape(-1), factor_rows.reshape(-1, side, rank), observed, columns
    )
    row_total = lax.psum(row_part.reshape(-1, rank), "cols")
    sums = block_sums(ids_here, line_exchange(parts, 3), SIDE * SIDE * held)
    sums = plane_exchange([a.reshape(SIDE, SIDE, held, *a.shape[1:]) for a in sums])
    cols_new = column_step(
        factor_cols.reshape(held, side, rank), [a.reshape(SIDE * SIDE, *a.shape[2:]) for a in sums]
    ).reshape(-1, rank)
    rows_new = factor_rows.astype(jnp.float32) - step_rate * row_total
    return (rows_new, cols_new)


def solution(mesh):
    return jax.shard_map(
        body,
        mesh=mesh,
        in_specs=(
            P("rows", None),
            P(("rows", "cols"), None),
            P(("rows", "cols"), None, None),
            P(("rows", "cols")),
            P(("rows", "cols"), None),
            P(("rows", "cols")),
        ),
        out_specs=(P("rows", None), P(("rows", "cols"), None)),
        check_vma=False,
    )
```

```python
import functools

import jax
import jax.numpy as jnp
from jax import lax
from jax.experimental import pallas as pl
from jax.experimental.pallas import tpu as pltpu
from jax.sharding import PartitionSpec as P

MESH = pl.DeviceIdType.MESH
step_rate = 0.02
smooth_width = 0.5
SIDE = 4
CORES = 2
STEP_TILES = 16
ROW_CUTS = ((0, 88), (88, 88), (176, 80))
BIN = 2 * SIDE * SIDE
CBD = 8


def position():
    rows = lax.axis_index("rows")
    return (
        lax.div(rows, SIDE * CORES),
        lax.rem(lax.div(rows, CORES), SIDE),
        lax.rem(rows, CORES),
        lax.axis_index("cols"),
    )


def device_at(y, x, core, z):
    return ((y * SIDE + x) * CORES + core, z)


AXES = (0, 1, 3)
ORDERS = ((0, 1, 3), (1, 3, 0), (3, 0, 1))


def request_kernel(ids_ref, v_ref, *refs):
    parts = len(ORDERS)
    ids_out, targets, held, ids_held = refs[0], refs[1 : parts + 1], refs[parts + 1 : 2 * parts + 1], refs[2 * parts + 1]
    own_sem, send_sem, recv_sem, slab_send, slab_recv, ids_send, ids_recv = refs[2 * parts + 2 :]
    me = position()

    def moved(axis, by, flip=0):
        there = list(me)
        there[axis] = lax.rem(there[axis] + (by + SIDE), SIDE)
        there[2] = 1 - me[2] if flip else me[2]
        return tuple(there)

    def bin_of(part, there):
        return there[ORDERS[part][0]] * CORES + there[2]

    loads, own = [], []
    for part, cut in enumerate(ROW_CUTS):
        _, first, second = ORDERS[part]
        line = part * CORES * SIDE + bin_of(part, me)
        loads.append(pltpu.make_async_copy(v_ref.at[:, pl.ds(*cut)], held[part], own_sem.at[part, 0]))
        own.append(pltpu.make_async_copy(held[part], targets[part].at[me[first], me[second]], own_sem.at[part, 1]))
        loads.append(pltpu.make_async_copy(ids_ref.at[line], ids_held.at[part], own_sem.at[part, 2]))
        own.append(pltpu.make_async_copy(ids_held.at[part], ids_out.at[line], own_sem.at[part, 3]))
    for copy in loads:
        copy.start()

    offsets = ((1, 0), (3, 0), (2, 0), (1, 1), (3, 1), (2, 1), (0, 1))
    greeted = [moved(axis, by, flip) for axis in AXES for by, flip in offsets[:-1]]
    greeted.append(moved(0, 0, 1))
    barrier = pltpu.get_barrier_semaphore()
    for there in greeted:
        pl.semaphore_signal(barrier, inc=1, device_id=device_at(*there), device_id_type=MESH)
    pl.semaphore_wait(barrier, len(greeted))
    for copy in loads:
        copy.wait()
    for copy in own:
        copy.start()

    def ask(part, place, start):
        by, flip = offsets[place]
        axis = ORDERS[part][0]
        to, source = moved(axis, by, flip), moved(axis, -by, flip)
        line = part * CORES * SIDE
        return pltpu.make_async_remote_copy(
            src_ref=ids_ref.at[line + bin_of(part, to)],
            dst_ref=ids_out.at[line + (bin_of(part, me) if start else bin_of(part, source))],
            send_sem=ids_send.at[part, place],
            recv_sem=ids_recv.at[part, place],
            device_id=device_at(*to),
            device_id_type=MESH,
        )

    def block(part, by_first, by_second, half=None):
        _, first, second = ORDERS[part]
        cut = pl.ds(0, CBD) if half is None else pl.ds(half * (CBD // 2), CBD // 2)
        return targets[part].at[moved(first, by_first)[first], moved(second, by_second)[second], cut]

    def near(part, axis, way, sems, target, source=None):
        send_sems, recv_sems, at = sems
        return pltpu.make_async_remote_copy(
            src_ref=target if source is None else source,
            dst_ref=target,
            send_sem=send_sems.at[at],
            recv_sem=recv_sems.at[at],
            device_id=device_at(*moved(ORDERS[part][axis], 1 if way == 0 else -1)),
            device_id_type=MESH,
        )

    def first_hop(part, step, way, by):
        sems = (send_sem, recv_sem, (part, step, way))
        own_block = held[part] if by == 0 else None
        return near(part, 1, way, sems, block(part, by, 0, None if step == 0 else way), own_block)

    def next_hop(part, place, step, way, by):
        sems = (slab_send, slab_recv, (part, place, step, way))
        own_block = held[part] if place == 0 and by == 0 else None
        return near(part, 2, way, sems, block(part, (0, -1, 1, 2)[place], by), own_block)

    back = (-1, 1)
    started = []

    def begin(copy):
        copy.start()
        started.append(copy)

    def hand_on(place):
        for part in range(parts):
            for way in (0, 1):
                begin(next_hop(part, place, 0, way, 0))

    for part in range(parts):
        for way in (0, 1):
            begin(first_hop(part, 0, way, 0))
    hand_on(0)
    for place in range(len(offsets)):
        for part in range(parts):
            begin(ask(part, place, True))
    for part in range(parts):
        for way in (0, 1):
            first_hop(part, 0, way, back[way]).wait_recv()
            begin(first_hop(part, 1, way, back[way]))
    hand_on(1)
    hand_on(2)
    for part in range(parts):
        for way in (0, 1):
            first_hop(part, 1, way, 2).wait_recv()
    hand_on(3)
    for place in range(SIDE):
        for part in range(parts):
            for way in (0, 1):
                next_hop(part, place, 0, way, back[way]).wait_recv()
                if place % 2 == way:
                    begin(next_hop(part, place, 1, way, back[way]))
    for place in range(SIDE):
        for part in range(parts):
            next_hop(part, place, 1, place % 2, 2).wait_recv()
    for place in range(len(offsets)):
        for part in range(parts):
            ask(part, place, False).wait_recv()
    for copy in own:
        copy.wait()
    for copy in started:
        copy.wait_send()


def request_blocks(ids, blocks):
    held, _, rank = blocks.shape
    parts = len(ROW_CUTS)
    spec = pl.BlockSpec(memory_space=pltpu.HBM)
    return pl.pallas_call(
        request_kernel,
        out_shape=(
            jax.ShapeDtypeStruct(ids.shape, ids.dtype),
            *(jax.ShapeDtypeStruct((SIDE, SIDE, held, size, rank), blocks.dtype) for _, size in ROW_CUTS),
        ),
        in_specs=[spec, spec],
        out_specs=(spec,) * (parts + 1),
        scratch_shapes=[pltpu.VMEM((held, size, rank), blocks.dtype) for _, size in ROW_CUTS]
        + [
            pltpu.VMEM((parts, *ids.shape[1:]), ids.dtype),
            pltpu.SemaphoreType.DMA((parts, 4)),
            pltpu.SemaphoreType.DMA((parts, 2, 2)),
            pltpu.SemaphoreType.DMA((parts, 2, 2)),
            pltpu.SemaphoreType.DMA((parts, SIDE, 2, 2)),
            pltpu.SemaphoreType.DMA((parts, SIDE, 2, 2)),
            pltpu.SemaphoreType.DMA((parts, 7)),
            pltpu.SemaphoreType.DMA((parts, 7)),
        ],
        compiler_params=pltpu.CompilerParams(collective_id=0, has_side_effects=True),
    )(ids, blocks)


def serve_kernel(ids, *refs):
    parts = len(ROW_CUTS)
    sources, targets = refs[:parts], refs[parts:]
    step = pl.program_id(0)
    bins = pl.num_programs(0)
    for part in range(parts):
        line = (part * bins + step) * 128

        def fill(place, carry, part=part, line=line):
            lanes = [place * 4 + turn for turn in range(4)]
            blocks = [sources[part][jnp.maximum(ids[line + lane], 0)] for lane in lanes]
            for lane, block in zip(lanes, blocks):
                targets[part][lane] = block
            return carry

        lax.fori_loop(0, lax.div(ids[line + BIN] + 3, 4), fill, 0)


def serve_blocks(ids, sources, slots):
    blocks, _, rank = sources[0].shape
    return pl.pallas_call(
        serve_kernel,
        out_shape=tuple(jax.ShapeDtypeStruct((slots, size, rank), jnp.bfloat16) for _, size in ROW_CUTS),
        grid_spec=pltpu.PrefetchScalarGridSpec(
            num_scalar_prefetch=1,
            grid=(slots // BIN,),
            in_specs=[
                pl.BlockSpec((blocks, size, rank), lambda i, *_: (0, 0, 0), pipeline_mode=pl.Buffered(1))
                for _, size in ROW_CUTS
            ],
            out_specs=tuple(pl.BlockSpec((BIN, size, rank), lambda i, *_: (i, 0, 0)) for _, size in ROW_CUTS),
        ),
        compiler_params=pltpu.CompilerParams(vmem_limit_bytes=60 << 20),
    )(ids, *sources)


def line_kernel(*refs):
    parts = len(ORDERS)
    sources, targets, held = refs[:parts], refs[parts : 2 * parts], refs[2 * parts : 3 * parts]
    own_sem, send_sem, recv_sem = refs[3 * parts :]
    me = position()
    offsets = ((1, 0), (3, 0), (2, 0), (1, 1), (3, 1), (2, 1), (0, 1))

    def moved(part, by, flip):
        there = list(me)
        axis = ORDERS[part][0]
        there[axis] = lax.rem(there[axis] + by, SIDE)
        there[2] = 1 - me[2] if flip else me[2]
        return tuple(there)

    def bin_of(part, there):
        return there[ORDERS[part][0]] * CORES + there[2]

    def slots(at):
        return pl.ds(pl.multiple_of(at * BIN, BIN), BIN)

    loads, copies = [], []
    for part in range(parts):
        here = bin_of(part, me)
        loads.append(pltpu.make_async_copy(sources[part].at[slots(here)], held[part], own_sem.at[part, 0]))
        copies.append(pltpu.make_async_copy(held[part], targets[part].at[slots(here)], own_sem.at[part, 1]))
    for copy in loads:
        copy.start()

    greeted = [moved(part, *offset) for part in range(parts) for offset in offsets[:-1]]
    greeted.append(moved(0, 0, 1))
    barrier = pltpu.get_barrier_semaphore()
    for there in greeted:
        pl.semaphore_signal(barrier, inc=1, device_id=device_at(*there), device_id_type=MESH)
    pl.semaphore_wait(barrier, len(greeted))

    def trade(part, place, start):
        by, flip = offsets[place]
        to, source = moved(part, by, flip), moved(part, SIDE - by if by else 0, flip)
        filled = bin_of(part, me) if start else bin_of(part, source)
        return pltpu.make_async_remote_copy(
            src_ref=sources[part].at[slots(bin_of(part, to))],
            dst_ref=targets[part].at[slots(filled)],
            send_sem=send_sem.at[part, place],
            recv_sem=recv_sem.at[part, place],
            device_id=device_at(*to),
            device_id_type=MESH,
        )

    for places in ((0, 1), (2,), (6,), (3, 4), (5,)):
        for part in range(parts):
            for place in places:
                trade(part, place, True).start()
    for load, copy in zip(loads, copies):
        load.wait()
        copy.start()
    for place in range(len(offsets)):
        for part in range(parts):
            trade(part, place, False).wait_recv()
            trade(part, place, True).wait_send()
    for copy in copies:
        copy.wait()


def line_exchange(sources, collective_id):
    spec = pl.BlockSpec(memory_space=pltpu.HBM)
    parts = len(sources)
    return pl.pallas_call(
        line_kernel,
        out_shape=tuple(jax.ShapeDtypeStruct(a.shape, a.dtype) for a in sources),
        in_specs=[spec] * parts,
        out_specs=(spec,) * parts,
        scratch_shapes=[pltpu.VMEM((BIN, *a.shape[1:]), a.dtype) for a in sources]
        + [pltpu.SemaphoreType.DMA((parts, 2))]
        + [pltpu.SemaphoreType.DMA((parts, 7))] * 2,
        compiler_params=pltpu.CompilerParams(collective_id=collective_id, has_side_effects=True),
    )(*sources)


def plane_kernel(*refs):
    parts = len(ORDERS)
    sources, targets, between = refs[:parts], refs[parts : 2 * parts], refs[2 * parts : 3 * parts]
    held, late_held = refs[3 * parts : 4 * parts], refs[4 * parts : 5 * parts]
    own_sem, late_sem, first_send, first_recv, then_send, then_recv = refs[5 * parts :]
    me = position()
    hops = (1, 3, 2)

    def moved(axis, by):
        there = list(me)
        there[axis] = lax.rem(there[axis] + by, SIDE)
        return tuple(there)

    loads, own = [], []
    for part in range(parts):
        at = me[ORDERS[part][1]]
        loads.append(pltpu.make_async_copy(sources[part].at[at], held[part], own_sem.at[part, 0]))
        own.append(pltpu.make_async_copy(held[part], between[part].at[at], own_sem.at[part, 1]))
    for copy in loads:
        copy.start()

    greeted = [moved(axis, by) for axis in AXES for by in hops]
    barrier = pltpu.get_barrier_semaphore()
    for there in greeted:
        pl.semaphore_signal(barrier, inc=1, device_id=device_at(*there), device_id_type=MESH)
    pl.semaphore_wait(barrier, len(greeted))

    def first(part, hop, turn, start):
        _, axis, last = ORDERS[part]
        by = hops[hop]
        to = moved(axis, by)
        filled = me[axis] if start else moved(axis, SIDE - by)[axis]
        row = lax.rem(me[last] + turn, SIDE)
        return pltpu.make_async_remote_copy(
            src_ref=sources[part].at[to[axis], row],
            dst_ref=between[part].at[filled, row],
            send_sem=first_send.at[part, hop, turn],
            recv_sem=first_recv.at[part, hop, turn],
            device_id=device_at(*to),
            device_id_type=MESH,
        )

    def then(part, hop, start):
        last = ORDERS[part][2]
        by = hops[hop]
        to = moved(last, by)
        filled = me[last] if start else moved(last, SIDE - by)[last]
        return pltpu.make_async_remote_copy(
            src_ref=between[part].at[:, to[last]],
            dst_ref=targets[part].at[:, filled],
            send_sem=then_send.at[part, hop],
            recv_sem=then_recv.at[part, hop],
            device_id=device_at(*to),
            device_id_type=MESH,
        )

    turns = hops + (0,)
    for turn in turns:
        for places in ((0, 1), (2,)):
            for part in range(parts):
                for hop in places:
                    first(part, hop, turn, True).start()
    for load, copy in zip(loads, own):
        load.wait()
        copy.start()
    for copy in own:
        copy.wait()
    for place, turn in enumerate(turns):
        for part in range(parts):
            for hop in range(len(hops)):
                first(part, hop, turn, False).wait_recv()
            if turn:
                then(part, place, True).start()
    late = []
    for part in range(parts):
        at = me[ORDERS[part][2]]
        load = pltpu.make_async_copy(between[part].at[:, at], late_held[part], late_sem.at[part, 0])
        load.start()
        copy = pltpu.make_async_copy(late_held[part], targets[part].at[:, at], late_sem.at[part, 1])
        late.append((load, copy))
    for load, copy in late:
        load.wait()
        copy.start()
    for part in range(parts):
        for hop in range(len(hops)):
            then(part, hop, False).wait_recv()
            then(part, hop, True).wait_send()
            for turn in turns:
                first(part, hop, turn, True).wait_send()
    for _, copy in late:
        copy.wait()


def plane_exchange(sums):
    spec = pl.BlockSpec(memory_space=pltpu.HBM)
    parts = len(sums)
    shapes = tuple(jax.ShapeDtypeStruct(a.shape, a.dtype) for a in sums)
    return pl.pallas_call(
        plane_kernel,
        out_shape=shapes * 2,
        in_specs=[spec] * parts,
        out_specs=(spec,) * (2 * parts),
        scratch_shapes=[pltpu.VMEM(a.shape[1:], a.dtype) for a in sums] * 2
        + [
            pltpu.SemaphoreType.DMA((parts, 2)),
            pltpu.SemaphoreType.DMA((parts, 2)),
            pltpu.SemaphoreType.DMA((parts, 3, SIDE)),
            pltpu.SemaphoreType.DMA((parts, 3, SIDE)),
            pltpu.SemaphoreType.DMA((parts, 3)),
            pltpu.SemaphoreType.DMA((parts, 3)),
        ],
        compiler_params=pltpu.CompilerParams(collective_id=2, has_side_effects=True),
    )(*sums)[:parts]


def tile_kernel(row_of, slot_of, u_ref, obs_ref, *refs):
    parts = len(ROW_CUTS)
    v_hbm, (rows_ref, *part_hbm) = refs[:parts], refs[parts : 2 * parts + 1]
    part_buf, v_buf = refs[2 * parts + 1 : 3 * parts + 1], refs[3 * parts + 1 : 4 * parts + 1]
    in_sem, out_sem = refs[4 * parts + 1 :]
    step = pl.program_id(0)
    steps = pl.num_programs(0)
    now = lax.rem(step, 2)
    tiles = steps * STEP_TILES

    def fetch(at, slot, lane):
        return [
            pltpu.make_async_copy(
                v_hbm[part].at[slot_of[part * tiles + at * STEP_TILES + lane]],
                v_buf[part].at[slot, lane],
                in_sem.at[part, slot, lane],
            )
            for part in range(parts)
        ]

    def put(at, slot, lane):
        return [
            pltpu.make_async_copy(
                part_buf[part].at[slot, lane],
                part_hbm[part].at[slot_of[part * tiles + at * STEP_TILES + lane]],
                out_sem.at[part, slot, lane],
            )
            for part in range(parts)
        ]

    @pl.when(step == 0)
    def _():
        rows_ref[...] = jnp.zeros_like(rows_ref)
        for lane in range(STEP_TILES):
            for copy in fetch(0, 0, lane):
                copy.start()

    @pl.when(step + 1 < steps)
    def _():
        for lane in range(STEP_TILES):
            for copy in fetch(step + 1, 1 - now, lane):
                copy.start()

    @pl.when(step >= 2)
    def _():
        for lane in range(STEP_TILES):
            for copy in put(step - 2, now, lane):
                copy.wait()

    for lane in range(STEP_TILES):
        for copy in fetch(step, now, lane):
            copy.wait()
    lanes = range(STEP_TILES)
    blocks = [row_of[step * STEP_TILES + lane] for lane in lanes]
    us = [u_ref[block] for block in blocks]
    vs = [jnp.concatenate([v_buf[part][now, lane] for part in range(parts)], axis=0) for lane in lanes]
    products = [
        lax.dot_general(u, v, (((1,), (1,)), ((), ())), preferred_element_type=jnp.float32)
        for u, v in zip(us, vs)
    ]
    slopes = []
    for lane in lanes:
        residual = products[lane] - obs_ref[lane].astype(jnp.float32)
        slopes.append(
            (residual * lax.rsqrt(residual * residual + smooth_width * smooth_width)).astype(jnp.bfloat16)
        )
    terms = [jnp.dot(slope, v, preferred_element_type=jnp.float32) for slope, v in zip(slopes, vs)]
    for lane in lanes:
        term = lax.dot_general(
            slopes[lane], us[lane], (((0,), (0,)), ((), ())), preferred_element_type=jnp.float32
        )
        for part, (low, size) in enumerate(ROW_CUTS):
            part_buf[part][now, lane] = term[low : low + size].astype(jnp.bfloat16)
    for block, term in zip(blocks, terms):
        rows_ref[block] += term
    for lane in range(STEP_TILES):
        for copy in put(step, now, lane):
            copy.start()

    @pl.when(step + 1 == steps)
    def _():
        for lane in range(STEP_TILES):
            for copy in put(step - 1, 1 - now, lane) + put(step, now, lane):
                copy.wait()


def tile_terms(row_of, slot_of, row_blocks, observed, col_parts):
    tiles, side, _ = observed.shape
    blocks, _, rank = row_blocks.shape
    parts, slots = len(ROW_CUTS), col_parts[0].shape[0]
    hbm = pl.BlockSpec(memory_space=pltpu.HBM)
    return pl.pallas_call(
        tile_kernel,
        out_shape=(
            jax.ShapeDtypeStruct((blocks, side, rank), jnp.float32),
            *(jax.ShapeDtypeStruct((slots, size, rank), jnp.bfloat16) for _, size in ROW_CUTS),
        ),
        grid_spec=pltpu.PrefetchScalarGridSpec(
            num_scalar_prefetch=2,
            grid=(tiles // STEP_TILES,),
            in_specs=[
                pl.BlockSpec((blocks, side, rank), lambda i, *_: (0, 0, 0)),
                pl.BlockSpec((STEP_TILES, side, side), lambda i, *_: (i, 0, 0)),
            ]
            + [hbm] * parts,
            out_specs=(pl.BlockSpec((blocks, side, rank), lambda i, *_: (0, 0, 0)),) + (hbm,) * parts,
            scratch_shapes=[pltpu.VMEM((2, STEP_TILES, size, rank), jnp.bfloat16) for _, size in ROW_CUTS * 2]
            + [
                pltpu.SemaphoreType.DMA((parts, 2, STEP_TILES)),
                pltpu.SemaphoreType.DMA((parts, 2, STEP_TILES)),
            ],
        ),
        compiler_params=pltpu.CompilerParams(vmem_limit_bytes=60 << 20),
        cost_estimate=pl.CostEstimate(
            flops=6 * tiles * side * side * rank, bytes_accessed=4 * tiles * side * side, transcendentals=0
        ),
    )(row_of, slot_of, row_blocks, observed, *col_parts)


def block_kernel(ids, *refs):
    parts = len(ROW_CUTS)
    sources, targets, totals = refs[:parts], refs[parts : 2 * parts], refs[2 * parts :]
    step = pl.program_id(0)
    bins = pl.num_programs(0)

    @pl.when(step == 0)
    def _():
        for total in totals:
            total[...] = jnp.zeros_like(total)

    lines = [(part * bins + step) * 128 for part in range(parts)]
    spare = targets[0].shape[0]

    def add(lane, carry):
        asked = [ids[line + lane] for line in lines]
        at = [jnp.where(block < 0, spare, block) for block in asked]
        sums = [totals[part][at[part]] + sources[part][lane].astype(jnp.float32) for part in range(parts)]
        for part in range(parts):
            totals[part][at[part]] = sums[part]
        return carry

    most = ids[lines[0] + BIN]
    for line in lines[1:]:
        most = jnp.maximum(most, ids[line + BIN])
    lax.fori_loop(0, most, add, 0)

    @pl.when(step + 1 == bins)
    def _():
        for part in range(parts):
            targets[part][...] = totals[part][pl.ds(0, spare)].astype(jnp.bfloat16)


def block_sums(ids, sources, blocks):
    rank = sources[0].shape[-1]
    whole = tuple((blocks, size, rank) for _, size in ROW_CUTS)
    return pl.pallas_call(
        block_kernel,
        out_shape=tuple(jax.ShapeDtypeStruct(shape, jnp.bfloat16) for shape in whole),
        grid_spec=pltpu.PrefetchScalarGridSpec(
            num_scalar_prefetch=1,
            grid=(sources[0].shape[0] // BIN,),
            in_specs=[pl.BlockSpec((BIN, size, rank), lambda i, *_: (i, 0, 0)) for _, size in ROW_CUTS],
            out_specs=tuple(
                pl.BlockSpec(shape, lambda i, *_: (0, 0, 0), pipeline_mode=pl.Buffered(1)) for shape in whole
            ),
            scratch_shapes=[pltpu.VMEM((blocks + 1, *shape[1:]), jnp.float32) for shape in whole],
        ),
        compiler_params=pltpu.CompilerParams(vmem_limit_bytes=60 << 20),
    )(ids, *sources)


def column_kernel(factor_ref, *refs):
    *sources, out_ref = refs
    factor = factor_ref[0].astype(jnp.float32)
    for (low, size), source in zip(ROW_CUTS, sources):
        total = source[0, 0].astype(jnp.float32)
        for sender in range(1, source.shape[0]):
            total += source[sender, 0].astype(jnp.float32)
        out_ref[0, pl.ds(low, size)] = factor[low : low + size] - step_rate * total


def column_step(factor, sums):
    held, side, rank = factor.shape
    block = pl.BlockSpec((1, side, rank), lambda i: (i, 0, 0))
    return pl.pallas_call(
        column_kernel,
        out_shape=jax.ShapeDtypeStruct(factor.shape, jnp.float32),
        grid=(held,),
        in_specs=[block]
        + [pl.BlockSpec((SIDE * SIDE, 1, size, rank), lambda i: (0, i, 0, 0)) for _, size in ROW_CUTS],
        out_specs=block,
        compiler_params=pltpu.CompilerParams(vmem_limit_bytes=60 << 20),
    )(factor, *sums)


def body(factor_rows, factor_cols, observed, tile_row, tile_owner, tile_sub):
    tiles, side, _ = observed.shape
    rank = factor_rows.shape[1]
    held = factor_cols.shape[0] // side
    owners = tile_owner[:, 0]
    spots = {
        0: owners // (SIDE * SIDE * CORES),
        1: owners // (SIDE * CORES) % SIDE,
        2: owners // SIDE % CORES,
        3: owners % SIDE,
    }
    bins = jnp.stack([spots[first] * CORES + spots[2] for first, _, _ in ORDERS])
    blocks = jnp.stack([(spots[second] * SIDE + spots[third]) * held + tile_sub for _, second, third in ORDERS])
    order = jnp.arange(tiles, dtype=jnp.int32)
    earlier = (bins[:, :, None] == bins[:, None, :]) & (order[None, None, :] < order[None, :, None])
    slot_of = bins * BIN + jnp.sum(earlier.astype(jnp.int32), axis=2)
    slots = CORES * SIDE * BIN
    place = jnp.arange(slots, dtype=jnp.int32)
    ids = jnp.max(
        jnp.where(slot_of[:, None, :] == place[None, :, None], blocks[:, None, :], -1), axis=2
    ).reshape(len(ORDERS) * CORES * SIDE, 1, BIN)
    filled = jnp.sum((ids >= 0).astype(jnp.int32), axis=2, keepdims=True)
    ids = jnp.concatenate([ids, jnp.broadcast_to(filled, (*filled.shape[:2], 128 - BIN))], axis=2)

    ids_here, *plane = request_blocks(ids, factor_cols.reshape(held, side, rank))
    ids_here = ids_here.reshape(-1)
    plane = [a.reshape(-1, *a.shape[3:]) for a in plane]
    columns = line_exchange(serve_blocks(ids_here, plane, slots), 1)
    row_part, *parts = tile_terms(
        tile_row, slot_of.reshape(-1), factor_rows.reshape(-1, side, rank), observed, columns
    )
    row_part, *back = lax.optimization_barrier((row_part, *line_exchange(parts, 3)))
    row_total = lax.psum(row_part.reshape(-1, rank), "cols")
    sums = block_sums(ids_here, back, SIDE * SIDE * held)
    sums = plane_exchange([a.reshape(SIDE, SIDE, held, *a.shape[1:]) for a in sums])
    cols_new = column_step(
        factor_cols.reshape(held, side, rank), [a.reshape(SIDE * SIDE, *a.shape[2:]) for a in sums]
    ).reshape(-1, rank)
    rows_new = factor_rows.astype(jnp.float32) - step_rate * row_total
    return (rows_new, cols_new)


def solution(mesh):
    return jax.shard_map(
        body,
        mesh=mesh,
        in_specs=(
            P("rows", None),
            P(("rows", "cols"), None),
            P(("rows", "cols"), None, None),
            P(("rows", "cols")),
            P(("rows", "cols"), None),
            P(("rows", "cols")),
        ),
        out_specs=(P("rows", None), P(("rows", "cols"), None)),
        check_vma=False,
    )
```

```python
import functools

import jax
import jax.numpy as jnp
from jax import lax
from jax.experimental import pallas as pl
from jax.experimental.pallas import tpu as pltpu
from jax.sharding import PartitionSpec as P

MESH = pl.DeviceIdType.MESH
step_rate = 0.02
smooth_width = 0.5
SIDE = 4
CORES = 2
STEP_TILES = 16
ROW_CUTS = ((0, 80), (80, 88), (168, 88))
BIN = 2 * SIDE * SIDE
CBD = 8


def position():
    rows = lax.axis_index("rows")
    return (
        lax.div(rows, SIDE * CORES),
        lax.rem(lax.div(rows, CORES), SIDE),
        lax.rem(rows, CORES),
        lax.axis_index("cols"),
    )


def device_at(y, x, core, z):
    return ((y * SIDE + x) * CORES + core, z)


AXES = (0, 1, 3)
ORDERS = ((0, 1, 3), (1, 3, 0), (3, 0, 1))


def request_kernel(ids_ref, v_ref, *refs):
    parts = len(ORDERS)
    ids_out, targets, held, ids_held = refs[0], refs[1 : parts + 1], refs[parts + 1 : 2 * parts + 1], refs[2 * parts + 1]
    own_sem, send_sem, recv_sem, slab_send, slab_recv, ids_send, ids_recv = refs[2 * parts + 2 :]
    me = position()

    def moved(axis, by, flip=0):
        there = list(me)
        there[axis] = lax.rem(there[axis] + (by + SIDE), SIDE)
        there[2] = 1 - me[2] if flip else me[2]
        return tuple(there)

    def bin_of(part, there):
        return there[ORDERS[part][0]] * CORES + there[2]

    loads, own = [], []
    for part, cut in enumerate(ROW_CUTS):
        _, first, second = ORDERS[part]
        line = part * CORES * SIDE + bin_of(part, me)
        loads.append(pltpu.make_async_copy(v_ref.at[:, pl.ds(*cut)], held[part], own_sem.at[part, 0]))
        own.append(pltpu.make_async_copy(held[part], targets[part].at[me[first], me[second]], own_sem.at[part, 1]))
        loads.append(pltpu.make_async_copy(ids_ref.at[line], ids_held.at[part], own_sem.at[part, 2]))
        own.append(pltpu.make_async_copy(ids_held.at[part], ids_out.at[line], own_sem.at[part, 3]))
    for copy in loads:
        copy.start()

    offsets = ((1, 0), (3, 0), (2, 0), (1, 1), (3, 1), (2, 1), (0, 1))
    greeted = [moved(axis, by, flip) for axis in AXES for by, flip in offsets[:-1]]
    greeted.append(moved(0, 0, 1))
    barrier = pltpu.get_barrier_semaphore()
    for there in greeted:
        pl.semaphore_signal(barrier, inc=1, device_id=device_at(*there), device_id_type=MESH)
    pl.semaphore_wait(barrier, len(greeted))
    for copy in loads:
        copy.wait()
    for copy in own:
        copy.start()

    def ask(part, place, start):
        by, flip = offsets[place]
        axis = ORDERS[part][0]
        to, source = moved(axis, by, flip), moved(axis, -by, flip)
        line = part * CORES * SIDE
        return pltpu.make_async_remote_copy(
            src_ref=ids_ref.at[line + bin_of(part, to)],
            dst_ref=ids_out.at[line + (bin_of(part, me) if start else bin_of(part, source))],
            send_sem=ids_send.at[part, place],
            recv_sem=ids_recv.at[part, place],
            device_id=device_at(*to),
            device_id_type=MESH,
        )

    def block(part, by_first, by_second, half=None):
        _, first, second = ORDERS[part]
        cut = pl.ds(0, CBD) if half is None else pl.ds(half * (CBD // 2), CBD // 2)
        return targets[part].at[moved(first, by_first)[first], moved(second, by_second)[second], cut]

    def near(part, axis, way, sems, target, source=None):
        send_sems, recv_sems, at = sems
        return pltpu.make_async_remote_copy(
            src_ref=target if source is None else source,
            dst_ref=target,
            send_sem=send_sems.at[at],
            recv_sem=recv_sems.at[at],
            device_id=device_at(*moved(ORDERS[part][axis], 1 if way == 0 else -1)),
            device_id_type=MESH,
        )

    def first_hop(part, step, way, by):
        sems = (send_sem, recv_sem, (part, step, way))
        own_block = held[part] if by == 0 else None
        return near(part, 1, way, sems, block(part, by, 0, None if step == 0 else way), own_block)

    def next_hop(part, place, step, way, by):
        sems = (slab_send, slab_recv, (part, place, step, way))
        own_block = held[part] if place == 0 and by == 0 else None
        return near(part, 2, way, sems, block(part, (0, -1, 1, 2)[place], by), own_block)

    back = (-1, 1)
    started = []

    def begin(copy):
        copy.start()
        started.append(copy)

    def hand_on(place):
        for part in range(parts):
            for way in (0, 1):
                begin(next_hop(part, place, 0, way, 0))

    for part in range(parts):
        for way in (0, 1):
            begin(first_hop(part, 0, way, 0))
    hand_on(0)
    for place in range(len(offsets)):
        for part in range(parts):
            begin(ask(part, place, True))
    for part in range(parts):
        for way in (0, 1):
            first_hop(part, 0, way, back[way]).wait_recv()
            begin(first_hop(part, 1, way, back[way]))
    hand_on(1)
    hand_on(2)
    for part in range(parts):
        for way in (0, 1):
            first_hop(part, 1, way, 2).wait_recv()
    hand_on(3)
    for place in range(SIDE):
        for part in range(parts):
            for way in (0, 1):
                next_hop(part, place, 0, way, back[way]).wait_recv()
                if place % 2 == way:
                    begin(next_hop(part, place, 1, way, back[way]))
    for place in range(SIDE):
        for part in range(parts):
            next_hop(part, place, 1, place % 2, 2).wait_recv()
    for place in range(len(offsets)):
        for part in range(parts):
            ask(part, place, False).wait_recv()
    for copy in own:
        copy.wait()
    for copy in started:
        copy.wait_send()


def request_blocks(ids, blocks):
    held, _, rank = blocks.shape
    parts = len(ROW_CUTS)
    spec = pl.BlockSpec(memory_space=pltpu.HBM)
    return pl.pallas_call(
        request_kernel,
        out_shape=(
            jax.ShapeDtypeStruct(ids.shape, ids.dtype),
            *(jax.ShapeDtypeStruct((SIDE, SIDE, held, size, rank), blocks.dtype) for _, size in ROW_CUTS),
        ),
        in_specs=[spec, spec],
        out_specs=(spec,) * (parts + 1),
        scratch_shapes=[pltpu.VMEM((held, size, rank), blocks.dtype) for _, size in ROW_CUTS]
        + [
            pltpu.VMEM((parts, *ids.shape[1:]), ids.dtype),
            pltpu.SemaphoreType.DMA((parts, 4)),
            pltpu.SemaphoreType.DMA((parts, 2, 2)),
            pltpu.SemaphoreType.DMA((parts, 2, 2)),
            pltpu.SemaphoreType.DMA((parts, SIDE, 2, 2)),
            pltpu.SemaphoreType.DMA((parts, SIDE, 2, 2)),
            pltpu.SemaphoreType.DMA((parts, 7)),
            pltpu.SemaphoreType.DMA((parts, 7)),
        ],
        compiler_params=pltpu.CompilerParams(collective_id=0, has_side_effects=True),
    )(ids, blocks)


def serve_kernel(ids, *refs):
    parts = len(ROW_CUTS)
    sources, targets = refs[:parts], refs[parts:]
    step = pl.program_id(0)
    bins = pl.num_programs(0)
    for part in range(parts):
        line = (part * bins + step) * 128

        def fill(place, carry, part=part, line=line):
            lanes = [place * 4 + turn for turn in range(4)]
            blocks = [sources[part][jnp.maximum(ids[line + lane], 0)] for lane in lanes]
            for lane, block in zip(lanes, blocks):
                targets[part][lane] = block
            return carry

        lax.fori_loop(0, lax.div(ids[line + BIN] + 3, 4), fill, 0)


def serve_blocks(ids, sources, slots):
    blocks, _, rank = sources[0].shape
    return pl.pallas_call(
        serve_kernel,
        out_shape=tuple(jax.ShapeDtypeStruct((slots, size, rank), jnp.bfloat16) for _, size in ROW_CUTS),
        grid_spec=pltpu.PrefetchScalarGridSpec(
            num_scalar_prefetch=1,
            grid=(slots // BIN,),
            in_specs=[
                pl.BlockSpec((blocks, size, rank), lambda i, *_: (0, 0, 0), pipeline_mode=pl.Buffered(1))
                for _, size in ROW_CUTS
            ],
            out_specs=tuple(pl.BlockSpec((BIN, size, rank), lambda i, *_: (i, 0, 0)) for _, size in ROW_CUTS),
        ),
        compiler_params=pltpu.CompilerParams(vmem_limit_bytes=60 << 20),
    )(ids, *sources)


def line_kernel(*refs):
    parts = len(ORDERS)
    sources, targets, held = refs[:parts], refs[parts : 2 * parts], refs[2 * parts : 3 * parts]
    own_sem, send_sem, recv_sem = refs[3 * parts :]
    me = position()
    offsets = ((1, 0), (3, 0), (2, 0), (1, 1), (3, 1), (2, 1), (0, 1))

    def moved(part, by, flip):
        there = list(me)
        axis = ORDERS[part][0]
        there[axis] = lax.rem(there[axis] + by, SIDE)
        there[2] = 1 - me[2] if flip else me[2]
        return tuple(there)

    def bin_of(part, there):
        return there[ORDERS[part][0]] * CORES + there[2]

    def slots(at):
        return pl.ds(pl.multiple_of(at * BIN, BIN), BIN)

    loads, copies = [], []
    for part in range(parts):
        here = bin_of(part, me)
        loads.append(pltpu.make_async_copy(sources[part].at[slots(here)], held[part], own_sem.at[part, 0]))
        copies.append(pltpu.make_async_copy(held[part], targets[part].at[slots(here)], own_sem.at[part, 1]))
    for copy in loads:
        copy.start()

    greeted = [moved(part, *offset) for part in range(parts) for offset in offsets[:-1]]
    greeted.append(moved(0, 0, 1))
    barrier = pltpu.get_barrier_semaphore()
    for there in greeted:
        pl.semaphore_signal(barrier, inc=1, device_id=device_at(*there), device_id_type=MESH)
    pl.semaphore_wait(barrier, len(greeted))

    def trade(part, place, start):
        by, flip = offsets[place]
        to, source = moved(part, by, flip), moved(part, SIDE - by if by else 0, flip)
        filled = bin_of(part, me) if start else bin_of(part, source)
        return pltpu.make_async_remote_copy(
            src_ref=sources[part].at[slots(bin_of(part, to))],
            dst_ref=targets[part].at[slots(filled)],
            send_sem=send_sem.at[part, place],
            recv_sem=recv_sem.at[part, place],
            device_id=device_at(*to),
            device_id_type=MESH,
        )

    for places in ((0, 1), (2,), (6,), (3, 4), (5,)):
        for part in range(parts):
            for place in places:
                trade(part, place, True).start()
    for load, copy in zip(loads, copies):
        load.wait()
        copy.start()
    for place in range(len(offsets)):
        for part in range(parts):
            trade(part, place, False).wait_recv()
            trade(part, place, True).wait_send()
    for copy in copies:
        copy.wait()


def line_exchange(sources, collective_id):
    spec = pl.BlockSpec(memory_space=pltpu.HBM)
    parts = len(sources)
    return pl.pallas_call(
        line_kernel,
        out_shape=tuple(jax.ShapeDtypeStruct(a.shape, a.dtype) for a in sources),
        in_specs=[spec] * parts,
        out_specs=(spec,) * parts,
        scratch_shapes=[pltpu.VMEM((BIN, *a.shape[1:]), a.dtype) for a in sources]
        + [pltpu.SemaphoreType.DMA((parts, 2))]
        + [pltpu.SemaphoreType.DMA((parts, 7))] * 2,
        compiler_params=pltpu.CompilerParams(collective_id=collective_id, has_side_effects=True),
    )(*sources)


def plane_kernel(*refs):
    parts = len(ORDERS)
    sources, targets, between = refs[:parts], refs[parts : 2 * parts], refs[2 * parts : 3 * parts]
    held, late_held = refs[3 * parts : 4 * parts], refs[4 * parts : 5 * parts]
    own_sem, late_sem, first_send, first_recv, then_send, then_recv = refs[5 * parts :]
    me = position()
    hops = (1, 3, 2)

    def moved(axis, by):
        there = list(me)
        there[axis] = lax.rem(there[axis] + by, SIDE)
        return tuple(there)

    loads, own = [], []
    for part in range(parts):
        at = me[ORDERS[part][1]]
        loads.append(pltpu.make_async_copy(sources[part].at[at], held[part], own_sem.at[part, 0]))
        own.append(pltpu.make_async_copy(held[part], between[part].at[at], own_sem.at[part, 1]))
    for copy in loads:
        copy.start()

    greeted = [moved(axis, by) for axis in AXES for by in hops]
    barrier = pltpu.get_barrier_semaphore()
    for there in greeted:
        pl.semaphore_signal(barrier, inc=1, device_id=device_at(*there), device_id_type=MESH)
    pl.semaphore_wait(barrier, len(greeted))

    def first(part, hop, turn, start):
        _, axis, last = ORDERS[part]
        by = hops[hop]
        to = moved(axis, by)
        filled = me[axis] if start else moved(axis, SIDE - by)[axis]
        row = lax.rem(me[last] + turn, SIDE)
        return pltpu.make_async_remote_copy(
            src_ref=sources[part].at[to[axis], row],
            dst_ref=between[part].at[filled, row],
            send_sem=first_send.at[part, hop, turn],
            recv_sem=first_recv.at[part, hop, turn],
            device_id=device_at(*to),
            device_id_type=MESH,
        )

    def then(part, hop, start):
        last = ORDERS[part][2]
        by = hops[hop]
        to = moved(last, by)
        filled = me[last] if start else moved(last, SIDE - by)[last]
        return pltpu.make_async_remote_copy(
            src_ref=between[part].at[:, to[last]],
            dst_ref=targets[part].at[:, filled],
            send_sem=then_send.at[part, hop],
            recv_sem=then_recv.at[part, hop],
            device_id=device_at(*to),
            device_id_type=MESH,
        )

    turns = hops + (0,)
    for turn in turns:
        for places in ((0, 1), (2,)):
            for part in range(parts):
                for hop in places:
                    first(part, hop, turn, True).start()
    for load, copy in zip(loads, own):
        load.wait()
        copy.start()
    for copy in own:
        copy.wait()
    for place, turn in enumerate(turns):
        for part in range(parts):
            for hop in range(len(hops)):
                first(part, hop, turn, False).wait_recv()
            if turn:
                then(part, place, True).start()
    late = []
    for part in range(parts):
        at = me[ORDERS[part][2]]
        load = pltpu.make_async_copy(between[part].at[:, at], late_held[part], late_sem.at[part, 0])
        load.start()
        copy = pltpu.make_async_copy(late_held[part], targets[part].at[:, at], late_sem.at[part, 1])
        late.append((load, copy))
    for load, copy in late:
        load.wait()
        copy.start()
    for part in range(parts):
        for hop in range(len(hops)):
            then(part, hop, False).wait_recv()
            then(part, hop, True).wait_send()
            for turn in turns:
                first(part, hop, turn, True).wait_send()
    for _, copy in late:
        copy.wait()


def plane_exchange(sums):
    spec = pl.BlockSpec(memory_space=pltpu.HBM)
    parts = len(sums)
    shapes = tuple(jax.ShapeDtypeStruct(a.shape, a.dtype) for a in sums)
    return pl.pallas_call(
        plane_kernel,
        out_shape=shapes * 2,
        in_specs=[spec] * parts,
        out_specs=(spec,) * (2 * parts),
        scratch_shapes=[pltpu.VMEM(a.shape[1:], a.dtype) for a in sums] * 2
        + [
            pltpu.SemaphoreType.DMA((parts, 2)),
            pltpu.SemaphoreType.DMA((parts, 2)),
            pltpu.SemaphoreType.DMA((parts, 3, SIDE)),
            pltpu.SemaphoreType.DMA((parts, 3, SIDE)),
            pltpu.SemaphoreType.DMA((parts, 3)),
            pltpu.SemaphoreType.DMA((parts, 3)),
        ],
        compiler_params=pltpu.CompilerParams(collective_id=2, has_side_effects=True),
    )(*sums)[:parts]


def tile_kernel(row_of, slot_of, u_ref, obs_ref, *refs):
    parts = len(ROW_CUTS)
    v_hbm, (rows_ref, *part_hbm) = refs[:parts], refs[parts : 2 * parts + 1]
    part_buf, v_buf = refs[2 * parts + 1 : 3 * parts + 1], refs[3 * parts + 1 : 4 * parts + 1]
    in_sem, out_sem = refs[4 * parts + 1 :]
    step = pl.program_id(0)
    steps = pl.num_programs(0)
    now = lax.rem(step, 2)
    tiles = steps * STEP_TILES

    def fetch(at, slot, lane):
        return [
            pltpu.make_async_copy(
                v_hbm[part].at[slot_of[part * tiles + at * STEP_TILES + lane]],
                v_buf[part].at[slot, lane],
                in_sem.at[part, slot, lane],
            )
            for part in range(parts)
        ]

    def put(at, slot, lane):
        return [
            pltpu.make_async_copy(
                part_buf[part].at[slot, lane],
                part_hbm[part].at[slot_of[part * tiles + at * STEP_TILES + lane]],
                out_sem.at[part, slot, lane],
            )
            for part in range(parts)
        ]

    @pl.when(step == 0)
    def _():
        rows_ref[...] = jnp.zeros_like(rows_ref)
        for lane in range(STEP_TILES):
            for copy in fetch(0, 0, lane):
                copy.start()

    @pl.when(step + 1 < steps)
    def _():
        for lane in range(STEP_TILES):
            for copy in fetch(step + 1, 1 - now, lane):
                copy.start()

    @pl.when(step >= 2)
    def _():
        for lane in range(STEP_TILES):
            for copy in put(step - 2, now, lane):
                copy.wait()

    for lane in range(STEP_TILES):
        for copy in fetch(step, now, lane):
            copy.wait()
    lanes = range(STEP_TILES)
    blocks = [row_of[step * STEP_TILES + lane] for lane in lanes]
    us = [u_ref[block] for block in blocks]
    vs = [jnp.concatenate([v_buf[part][now, lane] for part in range(parts)], axis=0) for lane in lanes]
    products = [
        lax.dot_general(u, v, (((1,), (1,)), ((), ())), preferred_element_type=jnp.float32)
        for u, v in zip(us, vs)
    ]
    slopes = []
    for lane in lanes:
        residual = products[lane] - obs_ref[lane].astype(jnp.float32)
        slopes.append(
            (residual * lax.rsqrt(residual * residual + smooth_width * smooth_width)).astype(jnp.bfloat16)
        )
    terms = [jnp.dot(slope, v, preferred_element_type=jnp.float32) for slope, v in zip(slopes, vs)]
    for lane in lanes:
        term = lax.dot_general(
            slopes[lane], us[lane], (((0,), (0,)), ((), ())), preferred_element_type=jnp.float32
        )
        for part, (low, size) in enumerate(ROW_CUTS):
            part_buf[part][now, lane] = term[low : low + size].astype(jnp.bfloat16)
    for block, term in zip(blocks, terms):
        rows_ref[block] += term
    for lane in range(STEP_TILES):
        for copy in put(step, now, lane):
            copy.start()

    @pl.when(step + 1 == steps)
    def _():
        for lane in range(STEP_TILES):
            for copy in put(step - 1, 1 - now, lane) + put(step, now, lane):
                copy.wait()


def tile_terms(row_of, slot_of, row_blocks, observed, col_parts):
    tiles, side, _ = observed.shape
    blocks, _, rank = row_blocks.shape
    parts, slots = len(ROW_CUTS), col_parts[0].shape[0]
    hbm = pl.BlockSpec(memory_space=pltpu.HBM)
    return pl.pallas_call(
        tile_kernel,
        out_shape=(
            jax.ShapeDtypeStruct((blocks, side, rank), jnp.float32),
            *(jax.ShapeDtypeStruct((slots, size, rank), jnp.bfloat16) for _, size in ROW_CUTS),
        ),
        grid_spec=pltpu.PrefetchScalarGridSpec(
            num_scalar_prefetch=2,
            grid=(tiles // STEP_TILES,),
            in_specs=[
                pl.BlockSpec((blocks, side, rank), lambda i, *_: (0, 0, 0)),
                pl.BlockSpec((STEP_TILES, side, side), lambda i, *_: (i, 0, 0)),
            ]
            + [hbm] * parts,
            out_specs=(pl.BlockSpec((blocks, side, rank), lambda i, *_: (0, 0, 0)),) + (hbm,) * parts,
            scratch_shapes=[pltpu.VMEM((2, STEP_TILES, size, rank), jnp.bfloat16) for _, size in ROW_CUTS * 2]
            + [
                pltpu.SemaphoreType.DMA((parts, 2, STEP_TILES)),
                pltpu.SemaphoreType.DMA((parts, 2, STEP_TILES)),
            ],
        ),
        compiler_params=pltpu.CompilerParams(vmem_limit_bytes=60 << 20),
        cost_estimate=pl.CostEstimate(
            flops=6 * tiles * side * side * rank, bytes_accessed=4 * tiles * side * side, transcendentals=0
        ),
    )(row_of, slot_of, row_blocks, observed, *col_parts)


def block_kernel(ids, *refs):
    parts = len(ROW_CUTS)
    sources, targets, totals = refs[:parts], refs[parts : 2 * parts], refs[2 * parts :]
    step = pl.program_id(0)
    bins = pl.num_programs(0)

    @pl.when(step == 0)
    def _():
        for total in totals:
            total[...] = jnp.zeros_like(total)

    lines = [(part * bins + step) * 128 for part in range(parts)]
    spare = targets[0].shape[0]

    def add(lane, carry):
        asked = [ids[line + lane] for line in lines]
        at = [jnp.where(block < 0, spare, block) for block in asked]
        sums = [totals[part][at[part]] + sources[part][lane].astype(jnp.float32) for part in range(parts)]
        for part in range(parts):
            totals[part][at[part]] = sums[part]
        return carry

    most = ids[lines[0] + BIN]
    for line in lines[1:]:
        most = jnp.maximum(most, ids[line + BIN])
    lax.fori_loop(0, most, add, 0)

    @pl.when(step + 1 == bins)
    def _():
        for part in range(parts):
            targets[part][...] = totals[part][pl.ds(0, spare)].astype(jnp.bfloat16)


def block_sums(ids, sources, blocks):
    rank = sources[0].shape[-1]
    whole = tuple((blocks, size, rank) for _, size in ROW_CUTS)
    return pl.pallas_call(
        block_kernel,
        out_shape=tuple(jax.ShapeDtypeStruct(shape, jnp.bfloat16) for shape in whole),
        grid_spec=pltpu.PrefetchScalarGridSpec(
            num_scalar_prefetch=1,
            grid=(sources[0].shape[0] // BIN,),
            in_specs=[pl.BlockSpec((BIN, size, rank), lambda i, *_: (i, 0, 0)) for _, size in ROW_CUTS],
            out_specs=tuple(
                pl.BlockSpec(shape, lambda i, *_: (0, 0, 0), pipeline_mode=pl.Buffered(1)) for shape in whole
            ),
            scratch_shapes=[pltpu.VMEM((blocks + 1, *shape[1:]), jnp.float32) for shape in whole],
        ),
        compiler_params=pltpu.CompilerParams(vmem_limit_bytes=60 << 20),
    )(ids, *sources)


def column_kernel(rows_ref, row_grad_ref, factor_ref, *refs):
    *sources, rows_out, out_ref = refs
    rows_out[...] = rows_ref[...].astype(jnp.float32) - step_rate * row_grad_ref[...]
    factor = factor_ref[0].astype(jnp.float32)
    for (low, size), source in zip(ROW_CUTS, sources):
        total = source[0, 0].astype(jnp.float32)
        for sender in range(1, source.shape[0]):
            total += source[sender, 0].astype(jnp.float32)
        out_ref[0, pl.ds(low, size)] = factor[low : low + size] - step_rate * total


def column_step(rows, row_grad, factor, sums):
    held, side, rank = factor.shape
    block = pl.BlockSpec((1, side, rank), lambda i: (i, 0, 0))
    return pl.pallas_call(
        column_kernel,
        out_shape=(jax.ShapeDtypeStruct(factor.shape, jnp.float32),) * 2,
        grid=(held,),
        in_specs=[block] * 3
        + [pl.BlockSpec((SIDE * SIDE, 1, size, rank), lambda i: (0, i, 0, 0)) for _, size in ROW_CUTS],
        out_specs=(block, block),
        compiler_params=pltpu.CompilerParams(vmem_limit_bytes=60 << 20),
    )(rows, row_grad, factor, *sums)


def body(factor_rows, factor_cols, observed, tile_row, tile_owner, tile_sub):
    tiles, side, _ = observed.shape
    rank = factor_rows.shape[1]
    held = factor_cols.shape[0] // side
    owners = tile_owner[:, 0]
    spots = {
        0: owners // (SIDE * SIDE * CORES),
        1: owners // (SIDE * CORES) % SIDE,
        2: owners // SIDE % CORES,
        3: owners % SIDE,
    }
    bins = jnp.stack([spots[first] * CORES + spots[2] for first, _, _ in ORDERS])
    blocks = jnp.stack([(spots[second] * SIDE + spots[third]) * held + tile_sub for _, second, third in ORDERS])
    order = jnp.arange(tiles, dtype=jnp.int32)
    earlier = (bins[:, :, None] == bins[:, None, :]) & (order[None, None, :] < order[None, :, None])
    slot_of = bins * BIN + jnp.sum(earlier.astype(jnp.int32), axis=2)
    slots = CORES * SIDE * BIN
    place = jnp.arange(slots, dtype=jnp.int32)
    ids = jnp.max(
        jnp.where(slot_of[:, None, :] == place[None, :, None], blocks[:, None, :], -1), axis=2
    ).reshape(len(ORDERS) * CORES * SIDE, 1, BIN)
    filled = jnp.sum((ids >= 0).astype(jnp.int32), axis=2, keepdims=True)
    ids = jnp.concatenate([ids, jnp.broadcast_to(filled, (*filled.shape[:2], 128 - BIN))], axis=2)

    ids_here, *plane = request_blocks(ids, factor_cols.reshape(held, side, rank))
    ids_here = ids_here.reshape(-1)
    plane = [a.reshape(-1, *a.shape[3:]) for a in plane]
    columns = line_exchange(serve_blocks(ids_here, plane, slots), 1)
    row_part, *parts = tile_terms(
        tile_row, slot_of.reshape(-1), factor_rows.reshape(-1, side, rank), observed, columns
    )
    row_part, *back = lax.optimization_barrier((row_part, *line_exchange(parts, 3)))
    row_total = lax.psum(row_part, "cols")
    sums = block_sums(ids_here, back, SIDE * SIDE * held)
    sums = plane_exchange([a.reshape(SIDE, SIDE, held, *a.shape[1:]) for a in sums])
    rows_new, cols_new = column_step(
        factor_rows.reshape(-1, side, rank),
        row_total,
        factor_cols.reshape(held, side, rank),
        [a.reshape(SIDE * SIDE, *a.shape[2:]) for a in sums],
    )
    return (rows_new.reshape(-1, rank), cols_new.reshape(-1, rank))


def solution(mesh):
    return jax.shard_map(
        body,
        mesh=mesh,
        in_specs=(
            P("rows", None),
            P(("rows", "cols"), None),
            P(("rows", "cols"), None, None),
            P(("rows", "cols")),
            P(("rows", "cols"), None),
            P(("rows", "cols")),
        ),
        out_specs=(P("rows", None), P(("rows", "cols"), None)),
        check_vma=False,
    )
```
